1024 devices in a mesh: dp: 16 (over z), shard: 64 (over x, y, core).
Axes of the slice: x: 4, y: 8, z: 16, core: 2. Of those that a mesh axis runs over, the one named last changes fastest.
Arguments:
- grads: bfloat16 [16, 512, 256, 256], P('dp', None, 'shard'), may hold values from -24 to 24
- owner_table: int32 [16, 128], replicated, may hold values from 0 to 31, as said below
- block_counts: int32 [16, 64], replicated, may hold values from 0 to 2, as said below
- prev_left: float32 [2048, 256, 256], P(('dp', 'shard')), as said below
- prev_right: float32 [2048, 256, 256], P(('dp', 'shard')), as said below
Outputs:
- updates: bfloat16 [512, 256, 256], P(None, 'shard')
The draws below stay inside these ranges and needn't reach their ends.
Inputs may be any that keep to these rules, and one draw needn't show every extreme that they name: `owner_table`: for group d and owner o, entries o * 2 to o * 2 + block_counts[d, o] - 1 of row d name blocks of the group, and these live entries together name each of the group's 32 blocks exactly once; the other entries name arbitrary blocks of the group. `block_counts`: each row sums to 32; in every row some owner has exactly 2 blocks. `prev_left`: each slot's matrix is symmetric positive semidefinite. `prev_right`: each slot's matrix is symmetric positive semidefinite.
All inputs are finite; a program needn't handle non-finite values.
Results may differ from the reference program's by a relative error of at most 0.02.
Values may be sent and summed in bfloat16 or wider, within the bound.
No kernel may reach another device: no remote copies, remote signals or barrier semaphores. Data moves between devices by JAX's collectives and lax.ppermute only.
A program may use at most 32 MiB of HBM per device.

```python
import jax
import jax.numpy as jnp
from jax import lax

BS = 256
CAP = 2
GROUPS = 16
OWNERS = 64
BPG = 32
NB = 512
SLOTS = 2048


def assignment(key):
    base = jax.random.fold_in(key, 7)

    def one_group(group_key):
        key_rank, key_force, key_perm, key_fill = jax.random.split(group_key, 4)
        slot_total = OWNERS * CAP
        slot_ids = jnp.arange(slot_total, dtype=jnp.int32)
        ranking = jax.random.permutation(key_rank, slot_total).astype(jnp.int32)
        forced = jax.random.randint(key_force, (), 0, OWNERS, dtype=jnp.int32)
        priority = jnp.where(slot_ids // CAP == forced, ranking - slot_total, ranking)
        ordering = jnp.argsort(priority, stable=True)
        placed = jnp.argsort(ordering, stable=True)
        chosen = (placed < BPG).astype(jnp.int32)
        counts = jnp.sum(chosen.reshape(OWNERS, CAP), axis=1).astype(jnp.int32)
        is_live = slot_ids % CAP < counts[slot_ids // CAP]
        position = jnp.cumsum(is_live.astype(jnp.int32)) - 1
        shuffled = jax.random.permutation(key_perm, BPG).astype(jnp.int32)
        filler = jax.random.randint(key_fill, (slot_total,), 0, BPG, dtype=jnp.int32)
        owner_rows = jnp.where(is_live, shuffled[jnp.clip(position, 0, BPG - 1)], filler)
        return (owner_rows.astype(jnp.int32), counts)
    return jax.vmap(one_group)(jax.random.split(base, GROUPS))


def draw_owner_table(key, part):
    return assignment(key)[0]


def draw_block_counts(key, part):
    return assignment(key)[1]


def draw_grads(key, part):
    base = jax.random.fold_in(key, 17)
    key_noise = jax.random.fold_in(base, 0)
    key_rows = jax.random.fold_in(base, 1)
    key_cols = jax.random.fold_in(base, 2)
    key_left = jax.random.fold_in(base, 4)
    key_right = jax.random.fold_in(base, 5)
    row_scale = 10.0 ** jax.random.uniform(key_rows, (NB, BS, 1), jnp.float32, -0.5, 0.5)
    col_scale = 10.0 ** jax.random.uniform(key_cols, (NB, 1, BS), jnp.float32, -0.5, 0.5)
    left_vec = jax.random.normal(key_left, (NB, BS, 1), jnp.float32)
    right_vec = jax.random.normal(key_right, (NB, 1, BS), jnp.float32)
    paired = left_vec * right_vec
    noise = jax.random.normal(key_noise, (GROUPS, NB, BS, BS), jnp.float32)
    values = 0.25 * noise + 0.18 / jnp.sqrt(jnp.float32(GROUPS)) * paired[None]
    return jnp.clip(values * row_scale * col_scale, -24.0, 24.0).astype(jnp.bfloat16)


def statistic(key, salt):
    base = jax.random.fold_in(key, salt)
    key_entries, key_rows, key_common = jax.random.split(base, 3)
    decades = 28.0
    entries = jax.random.normal(key_entries, (SLOTS, BS, BS), jnp.float32)
    shared = jax.random.normal(key_common, (SLOTS, 1, BS), jnp.float32)
    level_draw = jax.random.uniform(key_rows, (SLOTS, BS, 1), jnp.float32, 0.0, 1.0)
    row_scale = 10.0 ** (-0.5 * decades * level_draw)
    factor = (entries + 0.25 * shared) * row_scale
    gram_matrix = jnp.einsum('sik,sjk->sij', factor, factor, precision=lax.Precision.HIGHEST) / BS
    gram_matrix = 0.5 * (gram_matrix + jnp.swapaxes(gram_matrix, 1, 2))
    weight = 3.0 * BS * jnp.sqrt(jnp.float32(BS))
    return weight * gram_matrix


def draw_prev_left(key, part):
    return statistic(key, 11)


def draw_prev_right(key, part):
    return statistic(key, 13)


def setup_inputs(seed: int = 0) -> dict:
    seeds = jax.random.split(jax.random.key(seed), 6)
    grads = draw_grads(jax.random.fold_in(seeds[5], 71), 0)
    owner_table = draw_owner_table(jax.random.fold_in(seeds[5], 71), 0)
    block_counts = draw_block_counts(jax.random.fold_in(seeds[5], 71), 0)
    prev_left = draw_prev_left(jax.random.fold_in(seeds[5], 71), 0)
    prev_right = draw_prev_right(jax.random.fold_in(seeds[5], 71), 0)
    return dict(grads=grads, owner_table=owner_table, block_counts=block_counts, prev_left=prev_left, prev_right=prev_right)


stat_decay = 0.9
eps_small = 1e-06

def inverse_root(factor):
    size_now = factor.shape[0]
    unit_matrix = jnp.eye(size_now, dtype=jnp.float32)
    norm_scale = size_now * jnp.sqrt(jnp.mean(factor * factor) + eps_small)
    start = factor / norm_scale
    first = (1.25 * unit_matrix - 0.25 * start).astype(jnp.bfloat16)
    square = jnp.dot(first, first, preferred_element_type=jnp.float32).astype(jnp.bfloat16)
    fourth = jnp.dot(square, square, preferred_element_type=jnp.float32).astype(jnp.bfloat16)
    next_state = jnp.dot(fourth, start.astype(jnp.bfloat16), preferred_element_type=jnp.float32)
    second = (1.25 * unit_matrix - 0.25 * next_state).astype(jnp.bfloat16)
    return jnp.dot(first, second, preferred_element_type=jnp.float32).astype(jnp.bfloat16)

def precondition(grad_block, left_prev, right_prev):
    left_factor = stat_decay * left_prev + (1.0 - stat_decay) * jnp.dot(grad_block, grad_block.T, preferred_element_type=jnp.float32)
    right_factor = stat_decay * right_prev + (1.0 - stat_decay) * jnp.dot(grad_block.T, grad_block, preferred_element_type=jnp.float32)
    root_left = inverse_root(left_factor)
    root_right = inverse_root(right_factor)
    half_done = jnp.dot(root_left, grad_block, preferred_element_type=jnp.float32).astype(jnp.bfloat16)
    precond = jnp.dot(half_done, root_right, preferred_element_type=jnp.float32)
    grad_wide = grad_block.astype(jnp.float32)
    grad_norm = jnp.sqrt(jnp.mean(grad_wide * grad_wide) + eps_small)
    cond_norm = jnp.sqrt(jnp.mean(precond * precond) + eps_small)
    return (precond * (grad_norm / cond_norm)).astype(jnp.bfloat16)

def reference(grads, owner_table, block_counts, prev_left, prev_right):

    def add_replica(running, replica):
        return (running + replica.astype(jnp.float32), None)
    total, unused = lax.scan(add_replica, jnp.zeros(grads.shape[1:], jnp.float32), grads)
    summed = total.astype(jnp.bfloat16)
    slot_total = OWNERS * CAP
    slot_ids = jnp.arange(slot_total, dtype=jnp.int32)
    is_live = (slot_ids % CAP)[None, :] < block_counts[:, slot_ids // CAP]
    matches = (owner_table[:, None, :] == jnp.arange(BPG, dtype=jnp.int32)[None, :, None]) & is_live[:, None, :]
    earliest = lax.optimization_barrier(jnp.min(jnp.where(matches, slot_ids[None, None, :], slot_total), axis=2))
    has_slot = (earliest < slot_total).reshape(-1)
    earliest = jnp.minimum(earliest, slot_total - 1)
    group_ids = jnp.arange(GROUPS, dtype=jnp.int32)[:, None]
    stat_index = ((group_ids * OWNERS + earliest // CAP) * CAP + earliest % CAP).reshape(-1).astype(jnp.int32)

    def one_block(inputs):
        grad_block, index_now, present = inputs
        update = precondition(grad_block, prev_left[index_now], prev_right[index_now])
        return jnp.where(present, update, jnp.zeros_like(update))
    return lax.map(one_block, (summed, stat_index, has_slot))
```

```python
import jax
import jax.numpy as jnp
from jax import lax
from jax.sharding import PartitionSpec as P

CAP = 2


stat_decay = 0.9
eps_small = 1e-06


def inverse_root(factor):
    size_now = factor.shape[0]
    unit_matrix = jnp.eye(size_now, dtype=jnp.float32)
    norm_scale = size_now * jnp.sqrt(jnp.mean(factor * factor) + eps_small)
    start = factor / norm_scale
    first = (1.25 * unit_matrix - 0.25 * start).astype(jnp.bfloat16)
    square = jnp.dot(first, first, preferred_element_type=jnp.float32).astype(jnp.bfloat16)
    fourth = jnp.dot(square, square, preferred_element_type=jnp.float32).astype(jnp.bfloat16)
    next_state = jnp.dot(fourth, start.astype(jnp.bfloat16), preferred_element_type=jnp.float32)
    second = (1.25 * unit_matrix - 0.25 * next_state).astype(jnp.bfloat16)
    return jnp.dot(first, second, preferred_element_type=jnp.float32).astype(jnp.bfloat16)


def precondition(grad_block, left_prev, right_prev):
    left_factor = stat_decay * left_prev + (1.0 - stat_decay) * jnp.dot(
        grad_block, grad_block.T, preferred_element_type=jnp.float32
    )
    right_factor = stat_decay * right_prev + (1.0 - stat_decay) * jnp.dot(
        grad_block.T, grad_block, preferred_element_type=jnp.float32
    )
    root_left = inverse_root(left_factor)
    root_right = inverse_root(right_factor)
    half_done = jnp.dot(root_left, grad_block, preferred_element_type=jnp.float32).astype(
        jnp.bfloat16
    )
    precond = jnp.dot(half_done, root_right, preferred_element_type=jnp.float32)
    grad_wide = grad_block.astype(jnp.float32)
    grad_norm = jnp.sqrt(jnp.mean(grad_wide * grad_wide) + eps_small)
    cond_norm = jnp.sqrt(jnp.mean(precond * precond) + eps_small)
    return (precond * (grad_norm / cond_norm)).astype(jnp.bfloat16)


def refresh(arrived, prev_left, prev_right):
    return jax.vmap(precondition)(arrived, prev_left, prev_right)


def shifted(value, step):
    size = lax.axis_size("dp")
    return lax.ppermute(value, "dp", [(i, (i + step) % size) for i in range(size)])


def every_other(size):
    return [list(range(start, size, 2)) for start in range(2)]


def body(grads, owner_table, block_counts, prev_left, prev_right):
    owners = lax.axis_size("shard")
    groups = lax.axis_size("dp")
    my_group = lax.axis_index("dp")
    parity = my_group % 2
    blocks = grads.shape[1]
    row_count = grads.shape[2]
    block_width = grads.shape[3]
    per_group = blocks // groups
    half = per_group // 2
    slot_total = owners * CAP
    slot_ids = jnp.arange(slot_total, dtype=jnp.int32)
    my_table = lax.dynamic_index_in_dim(owner_table, my_group, 0, keepdims=False)
    my_counts = lax.dynamic_index_in_dim(block_counts, my_group, 0, keepdims=False)
    is_live = (slot_ids % CAP).reshape(owners, CAP) < my_counts[:, None]
    is_live = is_live.reshape(slot_total)
    matches = (
        my_table[None, :] == jnp.arange(per_group, dtype=jnp.int32)[:, None]
    ) & is_live[None, :]
    earliest = jnp.min(jnp.where(matches, slot_ids[None, :], slot_total), axis=1)
    has_slot = earliest < slot_total
    earliest = jnp.minimum(earliest, slot_total - 1)

    by_parity = grads.reshape(groups // 2, 2, per_group, row_count, block_width)
    mine = lax.dynamic_index_in_dim(by_parity, parity, 1, keepdims=False)
    other = lax.dynamic_index_in_dim(by_parity, 1 - parity, 1, keepdims=False)
    from_above = shifted(other[:, :half], -1)
    from_below = shifted(other[:, half:], 1)
    paired = mine.astype(jnp.float32) + jnp.concatenate(
        [from_above, from_below], axis=1
    ).astype(jnp.float32)
    parts = lax.all_to_all(
        paired.astype(jnp.bfloat16),
        "dp",
        0,
        0,
        tiled=True,
        axis_index_groups=every_other(groups),
    )
    summed = jnp.sum(parts.astype(jnp.float32), axis=0).astype(jnp.bfloat16)
    outgoing = jnp.take(summed, my_table, axis=0, mode="clip")
    arrived = lax.all_to_all(
        outgoing.reshape(owners, CAP, row_count, block_width), "shard", 0, 0, tiled=True
    )
    arrived = jnp.swapaxes(arrived, 0, 1).reshape(CAP, block_width, block_width)
    fresh = refresh(arrived, prev_left, prev_right)
    fresh = jnp.swapaxes(fresh.reshape(CAP, owners, row_count, block_width), 0, 1)
    returned = lax.all_to_all(fresh, "shard", 0, 0, tiled=True)
    chosen = jnp.take(
        returned.reshape(slot_total, row_count, block_width), earliest, axis=0, mode="clip"
    )
    chosen = jnp.where(has_slot[:, None, None], chosen, jnp.zeros_like(chosen))
    same = lax.all_gather(
        chosen, "dp", axis=0, tiled=False, axis_index_groups=every_other(groups)
    )
    from_below = shifted(same[:, :half], 1)
    from_above = shifted(same[:, half:], -1)
    opposite = jnp.concatenate([from_below, from_above], axis=1)
    even = jnp.where(parity == 0, same, opposite)
    odd = jnp.where(parity == 0, opposite, same)
    return jnp.stack([even, odd], axis=1).reshape(blocks, row_count, block_width)


def solution(mesh):
    return jax.shard_map(
        body,
        mesh=mesh,
        in_specs=(
            P("dp", None, "shard", None),
            P(),
            P(),
            P(("dp", "shard"), None, None),
            P(("dp", "shard"), None, None),
        ),
        out_specs=P(None, "shard", None),
        check_vma=False,
    )
```

```python
import jax
import jax.numpy as jnp
from jax import lax
from jax.experimental import pallas as pl
from jax.experimental.pallas import tpu as pltpu
from jax.sharding import PartitionSpec as P

CAP = 2
VMEM_GRANT = 12 * 1024 * 1024


stat_decay = 0.9
eps_small = 1e-06

ROWS_ROWS = (((1,), (1,)), ((), ()))
COLS_COLS = (((0,), (0,)), ((), ()))


def product(left, right, dims=(((1,), (0,)), ((), ()))):
    return lax.dot_general(left, right, dims, preferred_element_type=jnp.float32)


def mean_square(value):
    return jnp.sum(value * value, keepdims=True) * (1.0 / value.size)


def refresh_kernel(arrived_ref, left_ref, right_ref, fresh_ref):
    count, size_now, _ = arrived_ref.shape
    rows = lax.broadcasted_iota(jnp.int32, (size_now, size_now), 0)
    cols = lax.broadcasted_iota(jnp.int32, (size_now, size_now), 1)
    diagonal = jnp.where(rows == cols, 1.25, 0.0).astype(jnp.float32)
    grads = [arrived_ref[slot] for slot in range(count)]
    factors = []
    for slot, grad in enumerate(grads):
        factors.append(
            left_ref[slot] + (1.0 - stat_decay) * product(grad, grad, ROWS_ROWS)
        )
        factors.append(
            right_ref[slot] + (1.0 - stat_decay) * product(grad, grad, COLS_COLS)
        )
    scales = [1.0 / (size_now * jnp.sqrt(mean_square(a) + eps_small)) for a in factors]
    starts = [a * s for a, s in zip(factors, scales)]
    firsts = [(diagonal - 0.25 * s).astype(jnp.bfloat16) for s in starts]
    starts = [s.astype(jnp.bfloat16) for s in starts]
    squares = [product(f, f).astype(jnp.bfloat16) for f in firsts]
    fourths = [product(s, s).astype(jnp.bfloat16) for s in squares]
    states = [product(f, s) for f, s in zip(fourths, starts)]
    seconds = [(diagonal - 0.25 * s).astype(jnp.bfloat16) for s in states]
    roots = [product(f, s).astype(jnp.bfloat16) for f, s in zip(firsts, seconds)]
    halves = [
        product(roots[2 * slot], grad).astype(jnp.bfloat16) for slot, grad in enumerate(grads)
    ]
    finals = [product(h, roots[2 * slot + 1]) for slot, h in enumerate(halves)]
    for slot, (grad, final) in enumerate(zip(grads, finals)):
        wide = grad.astype(jnp.float32)
        grad_norm = jnp.sqrt(mean_square(wide) + eps_small)
        cond_norm = jnp.sqrt(mean_square(final) + eps_small)
        fresh_ref[slot] = (final * (grad_norm / cond_norm)).astype(jnp.bfloat16)


def refresh(arrived, prev_left, prev_right):
    count, size_now, _ = arrived.shape
    return pl.pallas_call(
        refresh_kernel,
        out_shape=jax.ShapeDtypeStruct(arrived.shape, jnp.bfloat16),
        cost_estimate=pl.CostEstimate(
            flops=24 * count * size_now**3,
            bytes_accessed=12 * count * size_now**2,
            transcendentals=0,
        ),
        compiler_params=pltpu.CompilerParams(vmem_limit_bytes=VMEM_GRANT),
        name="refresh",
    )(arrived, prev_left, prev_right)


def part_kernel(parity_ref, grads_ref, mine_ref, first_ref, second_ref, sems):
    parity = parity_ref[0]
    half = first_ref.shape[0]
    copies = [
        pltpu.make_async_copy(grads_ref.at[:half, 1 - parity], first_ref, sems.at[0]),
        pltpu.make_async_copy(grads_ref.at[half:, 1 - parity], second_ref, sems.at[1]),
        pltpu.make_async_copy(grads_ref.at[:, parity], mine_ref, sems.at[2]),
    ]
    for copy in copies:
        copy.start()
    for copy in copies:
        copy.wait()


def part(parity, by_parity):
    count = by_parity.shape[0]
    pieces = [
        jax.ShapeDtypeStruct((size,) + by_parity.shape[2:], jnp.bfloat16)
        for size in (count, count // 2, count // 2)
    ]
    return pl.pallas_call(
        part_kernel,
        in_specs=[pl.BlockSpec(memory_space=pltpu.SMEM), pl.BlockSpec(memory_space=pltpu.HBM)],
        out_shape=pieces,
        out_specs=[pl.BlockSpec(memory_space=pltpu.VMEM)] * 3,
        scratch_shapes=[pltpu.SemaphoreType.DMA((3,))],
        compiler_params=pltpu.CompilerParams(vmem_limit_bytes=VMEM_GRANT),
        name="part",
    )(parity, by_parity)


def pair_kernel(mine_ref, first_ref, second_ref, out_ref, sum_ref, sems):
    half = first_ref.shape[0]
    copies = []
    for index in range(2 * half):
        came_ref = first_ref if index < half else second_ref
        sum_ref[index] = (
            mine_ref[index].astype(jnp.float32) + came_ref[index % half].astype(jnp.float32)
        ).astype(jnp.bfloat16)
        copies.append(
            pltpu.make_async_copy(sum_ref.at[index], out_ref.at[index], sems.at[index])
        )
        copies[-1].start()
    for copy in copies:
        copy.wait()


def pair(mine, first, second):
    return pl.pallas_call(
        pair_kernel,
        in_specs=[pl.BlockSpec(memory_space=pltpu.VMEM)] * 3,
        out_specs=pl.BlockSpec(memory_space=pl.ANY),
        out_shape=jax.ShapeDtypeStruct(mine.shape, jnp.bfloat16),
        scratch_shapes=[
            pltpu.VMEM(mine.shape, jnp.bfloat16),
            pltpu.SemaphoreType.DMA((mine.shape[0],)),
        ],
        compiler_params=pltpu.CompilerParams(vmem_limit_bytes=VMEM_GRANT),
        name="pair",
    )(mine, first, second)


def gather_rows_kernel(table_ref, parts_ref, out_ref, sum_ref):
    total = parts_ref[0].astype(jnp.float32)
    for part in range(1, parts_ref.shape[0]):
        total += parts_ref[part].astype(jnp.float32)
    sum_ref[...] = total.astype(jnp.bfloat16)

    def step(slot, carry):
        out_ref[slot] = sum_ref[table_ref[slot]]
        return carry

    lax.fori_loop(0, out_ref.shape[0], step, 0, unroll=8)


def sum_and_gather(table, parts):
    count = table.shape[0]
    return pl.pallas_call(
        gather_rows_kernel,
        in_specs=[
            pl.BlockSpec(memory_space=pltpu.SMEM),
            pl.BlockSpec(memory_space=pltpu.VMEM),
        ],
        out_shape=jax.ShapeDtypeStruct((count,) + parts.shape[2:], jnp.bfloat16),
        scratch_shapes=[pltpu.VMEM(parts.shape[1:], jnp.bfloat16)],
        compiler_params=pltpu.CompilerParams(vmem_limit_bytes=VMEM_GRANT),
        name="sum_and_gather",
    )(table, parts)


def choose_kernel(picks_ref, returned_ref, chosen_ref):
    for block in range(chosen_ref.shape[0]):
        pick = picks_ref[block]
        found = returned_ref[jnp.maximum(pick, 0)]
        chosen_ref[block] = jnp.where(pick >= 0, found, jnp.zeros_like(found))


def choose(picks, returned):
    return pl.pallas_call(
        choose_kernel,
        in_specs=[
            pl.BlockSpec(memory_space=pltpu.SMEM),
            pl.BlockSpec(memory_space=pltpu.VMEM),
        ],
        out_shape=jax.ShapeDtypeStruct(picks.shape + returned.shape[1:], jnp.bfloat16),
        compiler_params=pltpu.CompilerParams(vmem_limit_bytes=VMEM_GRANT),
        name="choose",
    )(picks, returned)


def place_kernel(parity_ref, same_ref, low_ref, high_ref, out_ref, sems):
    parity = parity_ref[0]
    half = low_ref.shape[0]
    copies = [
        pltpu.make_async_copy(same_ref, out_ref.at[:, parity], sems.at[0]),
        pltpu.make_async_copy(low_ref, out_ref.at[:half, 1 - parity], sems.at[1]),
        pltpu.make_async_copy(high_ref, out_ref.at[half:, 1 - parity], sems.at[2]),
    ]
    for copy in copies:
        copy.start()
    for copy in copies:
        copy.wait()


def place(parity, same, low, high):
    return pl.pallas_call(
        place_kernel,
        in_specs=[pl.BlockSpec(memory_space=pltpu.SMEM)]
        + [pl.BlockSpec(memory_space=pltpu.VMEM)] * 3,
        out_specs=pl.BlockSpec(memory_space=pl.ANY),
        out_shape=jax.ShapeDtypeStruct((same.shape[0], 2) + same.shape[1:], jnp.bfloat16),
        scratch_shapes=[pltpu.SemaphoreType.DMA((3,))],
        compiler_params=pltpu.CompilerParams(vmem_limit_bytes=VMEM_GRANT),
        name="place",
    )(parity, same, low, high)


def shifted(value, step):
    size = lax.axis_size("dp")
    return lax.ppermute(value, "dp", [(i, (i + step) % size) for i in range(size)])


def every_other(size):
    return [list(range(start, size, 2)) for start in range(2)]


def body(grads, owner_table, block_counts, prev_left, prev_right):
    owners = lax.axis_size("shard")
    groups = lax.axis_size("dp")
    my_group = lax.axis_index("dp")
    parity = my_group % 2
    blocks = grads.shape[1]
    row_count = grads.shape[2]
    block_width = grads.shape[3]
    per_group = blocks // groups
    half = groups // 4
    slot_total = owners * CAP
    slot_ids = jnp.arange(slot_total, dtype=jnp.int32)
    my_table = lax.dynamic_index_in_dim(owner_table, my_group, 0, keepdims=False)
    my_counts = lax.dynamic_index_in_dim(block_counts, my_group, 0, keepdims=False)
    is_live = (slot_ids % CAP).reshape(owners, CAP) < my_counts[:, None]
    is_live = is_live.reshape(slot_total)
    matches = (
        my_table[None, :] == jnp.arange(per_group, dtype=jnp.int32)[:, None]
    ) & is_live[None, :]
    earliest = jnp.min(jnp.where(matches, slot_ids[None, :], slot_total), axis=1)
    picks = jnp.where(earliest < slot_total, earliest, -1)

    by_parity = grads.reshape(groups // 2, 2, per_group, row_count, block_width)
    mine, first, second = part(parity.reshape(1), by_parity)
    paired = pair(mine, shifted(first, -1), shifted(second, 1))
    parts = lax.all_to_all(
        paired,
        "dp",
        0,
        0,
        tiled=True,
        axis_index_groups=every_other(groups),
    )
    outgoing = sum_and_gather(my_table, parts)
    arrived = lax.all_to_all(
        outgoing.reshape(owners, CAP, row_count, block_width), "shard", 0, 0, tiled=True
    )
    arrived = jnp.swapaxes(arrived, 0, 1).reshape(CAP, block_width, block_width)
    fresh = refresh(arrived, stat_decay * prev_left, stat_decay * prev_right)
    fresh = jnp.swapaxes(fresh.reshape(CAP, owners, row_count, block_width), 0, 1)
    returned = lax.all_to_all(fresh, "shard", 0, 0, tiled=True)
    chosen = choose(picks, returned.reshape(slot_total, row_count, block_width))
    same = lax.all_gather(
        chosen, "dp", axis=0, tiled=False, axis_index_groups=every_other(groups)
    )
    low = shifted(same[:half], 1)
    high = shifted(same[half:], -1)
    placed = place(parity.reshape(1), same, low, high)
    return placed.reshape(blocks, row_count, block_width)


def solution(mesh):
    return jax.shard_map(
        body,
        mesh=mesh,
        in_specs=(
            P("dp", None, "shard", None),
            P(),
            P(),
            P(("dp", "shard"), None, None),
            P(("dp", "shard"), None, None),
        ),
        out_specs=P(None, "shard", None),
        check_vma=False,
    )
```

```python
import jax
import jax.numpy as jnp
from jax import lax
from jax.experimental import pallas as pl
from jax.experimental.pallas import tpu as pltpu
from jax.sharding import PartitionSpec as P

CAP = 2
VMEM_GRANT = 12 * 1024 * 1024


stat_decay = 0.9
eps_small = 1e-06

ROWS_ROWS = (((1,), (1,)), ((), ()))
COLS_COLS = (((0,), (0,)), ((), ()))


def product(left, right, dims=(((1,), (0,)), ((), ()))):
    return lax.dot_general(left, right, dims, preferred_element_type=jnp.float32)


def mean_square(value):
    return jnp.sum(value * value, keepdims=True) * (1.0 / value.size)


def refresh_kernel(arrived_ref, left_ref, right_ref, fresh_ref):
    count, size_now, _ = arrived_ref.shape
    rows = lax.broadcasted_iota(jnp.int32, (size_now, size_now), 0)
    cols = lax.broadcasted_iota(jnp.int32, (size_now, size_now), 1)
    diagonal = jnp.where(rows == cols, 1.25, 0.0).astype(jnp.float32)
    grads = [arrived_ref[slot] for slot in range(count)]
    factors = []
    for slot, grad in enumerate(grads):
        factors.append(
            left_ref[slot] + (1.0 - stat_decay) * product(grad, grad, ROWS_ROWS)
        )
        factors.append(
            right_ref[slot] + (1.0 - stat_decay) * product(grad, grad, COLS_COLS)
        )
    scales = [1.0 / (size_now * jnp.sqrt(mean_square(a) + eps_small)) for a in factors]
    starts = [a * s for a, s in zip(factors, scales)]
    firsts = [(diagonal - 0.25 * s).astype(jnp.bfloat16) for s in starts]
    starts = [s.astype(jnp.bfloat16) for s in starts]
    squares = [product(f, f).astype(jnp.bfloat16) for f in firsts]
    fourths = [product(s, s).astype(jnp.bfloat16) for s in squares]
    states = [product(f, s) for f, s in zip(fourths, starts)]
    seconds = [(diagonal - 0.25 * s).astype(jnp.bfloat16) for s in states]
    roots = [product(f, s).astype(jnp.bfloat16) for f, s in zip(firsts, seconds)]
    halves = [
        product(roots[2 * slot], grad).astype(jnp.bfloat16) for slot, grad in enumerate(grads)
    ]
    finals = [product(h, roots[2 * slot + 1]) for slot, h in enumerate(halves)]
    for slot, (grad, final) in enumerate(zip(grads, finals)):
        wide = grad.astype(jnp.float32)
        grad_norm = jnp.sqrt(mean_square(wide) + eps_small)
        cond_norm = jnp.sqrt(mean_square(final) + eps_small)
        fresh_ref[slot] = (final * (grad_norm / cond_norm)).astype(jnp.bfloat16)


def refresh(arrived, prev_left, prev_right):
    count, size_now, _ = arrived.shape
    return pl.pallas_call(
        refresh_kernel,
        out_shape=jax.ShapeDtypeStruct(arrived.shape, jnp.bfloat16),
        cost_estimate=pl.CostEstimate(
            flops=24 * count * size_now**3,
            bytes_accessed=12 * count * size_now**2,
            transcendentals=0,
        ),
        compiler_params=pltpu.CompilerParams(vmem_limit_bytes=VMEM_GRANT),
        name="refresh",
    )(arrived, prev_left, prev_right)


def part_kernel(parity_ref, grads_ref, mine_ref, first_ref, second_ref, sems):
    parity = parity_ref[0]
    half = first_ref.shape[0]
    copies = [
        pltpu.make_async_copy(grads_ref.at[:half, 1 - parity], first_ref, sems.at[0]),
        pltpu.make_async_copy(grads_ref.at[half:, 1 - parity], second_ref, sems.at[1]),
        pltpu.make_async_copy(grads_ref.at[:, parity], mine_ref, sems.at[2]),
    ]
    for copy in copies:
        copy.start()
    for copy in copies:
        copy.wait()


def part(parity, by_parity):
    count = by_parity.shape[0]
    pieces = [
        jax.ShapeDtypeStruct((size,) + by_parity.shape[2:], jnp.bfloat16)
        for size in (count, count // 2, count // 2)
    ]
    return pl.pallas_call(
        part_kernel,
        in_specs=[pl.BlockSpec(memory_space=pltpu.SMEM), pl.BlockSpec(memory_space=pltpu.HBM)],
        out_shape=pieces,
        out_specs=[pl.BlockSpec(memory_space=pltpu.VMEM)] * 3,
        scratch_shapes=[pltpu.SemaphoreType.DMA((3,))],
        compiler_params=pltpu.CompilerParams(vmem_limit_bytes=VMEM_GRANT),
        name="part",
    )(parity, by_parity)


def pair_kernel(mine_ref, first_ref, second_ref, out_ref, sum_ref, sems):
    half = first_ref.shape[0]
    copies = []
    for index in range(2 * half):
        came_ref = first_ref if index < half else second_ref
        sum_ref[index] = (
            mine_ref[index].astype(jnp.float32) + came_ref[index % half].astype(jnp.float32)
        ).astype(jnp.bfloat16)
        copies.append(
            pltpu.make_async_copy(sum_ref.at[index], out_ref.at[index], sems.at[index])
        )
        copies[-1].start()
    for copy in copies:
        copy.wait()


def pair(mine, first, second):
    return pl.pallas_call(
        pair_kernel,
        in_specs=[pl.BlockSpec(memory_space=pltpu.VMEM)] * 3,
        out_specs=pl.BlockSpec(memory_space=pl.ANY),
        out_shape=jax.ShapeDtypeStruct(mine.shape, jnp.bfloat16),
        scratch_shapes=[
            pltpu.VMEM(mine.shape, jnp.bfloat16),
            pltpu.SemaphoreType.DMA((mine.shape[0],)),
        ],
        compiler_params=pltpu.CompilerParams(vmem_limit_bytes=VMEM_GRANT),
        name="pair",
    )(mine, first, second)


def gather_rows_kernel(table_ref, parts_ref, out_ref, sum_ref):
    total = parts_ref[0].astype(jnp.float32)
    for part in range(1, parts_ref.shape[0]):
        total += parts_ref[part].astype(jnp.float32)
    sum_ref[...] = total.astype(jnp.bfloat16)

    def step(slot, carry):
        out_ref[slot] = sum_ref[table_ref[slot]]
        return carry

    lax.fori_loop(0, out_ref.shape[0], step, 0, unroll=8)


def sum_and_gather(table, parts):
    count = table.shape[0]
    return pl.pallas_call(
        gather_rows_kernel,
        in_specs=[
            pl.BlockSpec(memory_space=pltpu.SMEM),
            pl.BlockSpec(memory_space=pltpu.VMEM),
        ],
        out_shape=jax.ShapeDtypeStruct((count,) + parts.shape[2:], jnp.bfloat16),
        scratch_shapes=[pltpu.VMEM(parts.shape[1:], jnp.bfloat16)],
        compiler_params=pltpu.CompilerParams(vmem_limit_bytes=VMEM_GRANT),
        name="sum_and_gather",
    )(table, parts)


def choose_kernel(picks_ref, returned_ref, chosen_ref):
    for block in range(chosen_ref.shape[0]):
        pick = picks_ref[block]
        found = returned_ref[jnp.maximum(pick, 0)]
        chosen_ref[block] = jnp.where(pick >= 0, found, jnp.zeros_like(found))


def choose(picks, returned):
    return pl.pallas_call(
        choose_kernel,
        in_specs=[
            pl.BlockSpec(memory_space=pltpu.SMEM),
            pl.BlockSpec(memory_space=pltpu.VMEM),
        ],
        out_shape=jax.ShapeDtypeStruct(picks.shape + returned.shape[1:], jnp.bfloat16),
        compiler_params=pltpu.CompilerParams(vmem_limit_bytes=VMEM_GRANT),
        name="choose",
    )(picks, returned)


def place_kernel(parity_ref, same_ref, low_ref, high_ref, out_ref, sems):
    parity = parity_ref[0]
    half = low_ref.shape[0]
    copies = [
        pltpu.make_async_copy(same_ref, out_ref.at[:, parity], sems.at[0]),
        pltpu.make_async_copy(low_ref, out_ref.at[:half, 1 - parity], sems.at[1]),
        pltpu.make_async_copy(high_ref, out_ref.at[half:, 1 - parity], sems.at[2]),
    ]
    for copy in copies:
        copy.start()
    for copy in copies:
        copy.wait()


def place(parity, same, low, high):
    return pl.pallas_call(
        place_kernel,
        in_specs=[pl.BlockSpec(memory_space=pltpu.SMEM)]
        + [pl.BlockSpec(memory_space=pltpu.VMEM)] * 3,
        out_specs=pl.BlockSpec(memory_space=pl.ANY),
        out_shape=jax.ShapeDtypeStruct((same.shape[0], 2) + same.shape[1:], jnp.bfloat16),
        scratch_shapes=[pltpu.SemaphoreType.DMA((3,))],
        compiler_params=pltpu.CompilerParams(vmem_limit_bytes=VMEM_GRANT),
        name="place",
    )(parity, same, low, high)


def shifted(value, step):
    size = lax.axis_size("dp")
    return lax.ppermute(value, "dp", [(i, (i + step) % size) for i in range(size)])


def every_other(size):
    return [list(range(start, size, 2)) for start in range(2)]


def body(grads, owner_table, block_counts, prev_left, prev_right):
    owners = lax.axis_size("shard")
    groups = lax.axis_size("dp")
    my_group = lax.axis_index("dp")
    parity = my_group % 2
    blocks = grads.shape[1]
    row_count = grads.shape[2]
    block_width = grads.shape[3]
    per_group = blocks // groups
    half = groups // 4
    slot_total = owners * CAP
    slot_ids = jnp.arange(slot_total, dtype=jnp.int32)
    my_table = lax.dynamic_index_in_dim(owner_table, my_group, 0, keepdims=False)
    my_counts = lax.dynamic_index_in_dim(block_counts, my_group, 0, keepdims=False)
    is_live = (slot_ids % CAP).reshape(owners, CAP) < my_counts[:, None]
    is_live = is_live.reshape(slot_total)
    matches = (
        my_table[None, :] == jnp.arange(per_group, dtype=jnp.int32)[:, None]
    ) & is_live[None, :]
    earliest = jnp.min(jnp.where(matches, slot_ids[None, :], slot_total), axis=1)
    picks = jnp.where(earliest < slot_total, earliest, -1)

    by_parity = grads.reshape(groups // 2, 2, per_group, row_count, block_width)
    mine, first, second = part(parity.reshape(1), by_parity)
    first, second, my_table, picks, old_left, old_right = lax.optimization_barrier(
        (
            shifted(first, -1),
            shifted(second, 1),
            my_table,
            picks,
            stat_decay * prev_left,
            stat_decay * prev_right,
        )
    )
    paired = pair(mine, first, second)
    parts = lax.all_to_all(
        paired,
        "dp",
        0,
        0,
        tiled=True,
        axis_index_groups=every_other(groups),
    )
    outgoing = sum_and_gather(my_table, parts)
    arrived = lax.all_to_all(
        outgoing.reshape(owners, CAP, row_count, block_width), "shard", 0, 0, tiled=True
    )
    arrived = jnp.swapaxes(arrived, 0, 1).reshape(CAP, block_width, block_width)
    fresh = refresh(arrived, old_left, old_right)
    fresh = jnp.swapaxes(fresh.reshape(CAP, owners, row_count, block_width), 0, 1)
    returned = lax.all_to_all(fresh, "shard", 0, 0, tiled=True)
    chosen = choose(picks, returned.reshape(slot_total, row_count, block_width))
    same = lax.all_gather(
        chosen, "dp", axis=0, tiled=False, axis_index_groups=every_other(groups)
    )
    low = shifted(same[:half], 1)
    high = shifted(same[half:], -1)
    placed = place(parity.reshape(1), same, low, high)
    return placed.reshape(blocks, row_count, block_width)


def solution(mesh):
    return jax.shard_map(
        body,
        mesh=mesh,
        in_specs=(
            P("dp", None, "shard", None),
            P(),
            P(),
            P(("dp", "shard"), None, None),
            P(("dp", "shard"), None, None),
        ),
        out_specs=P(None, "shard", None),
        check_vma=False,
    )
```

```python
import jax
import jax.numpy as jnp
from jax import lax
from jax.experimental import pallas as pl
from jax.experimental.pallas import tpu as pltpu
from jax.sharding import PartitionSpec as P

CAP = 2
RADIX = 4
VMEM_GRANT = 12 * 1024 * 1024


stat_decay = 0.9
eps_small = 1e-06

ROWS_ROWS = (((1,), (1,)), ((), ()))
COLS_COLS = (((0,), (0,)), ((), ()))


def product(left, right, dims=(((1,), (0,)), ((), ()))):
    return lax.dot_general(left, right, dims, preferred_element_type=jnp.float32)


def mean_square(value):
    return jnp.sum(value * value, keepdims=True) * (1.0 / value.size)


def refresh_kernel(arrived_ref, left_ref, right_ref, fresh_ref):
    count, size_now, _ = arrived_ref.shape
    rows = lax.broadcasted_iota(jnp.int32, (size_now, size_now), 0)
    cols = lax.broadcasted_iota(jnp.int32, (size_now, size_now), 1)
    diagonal = jnp.where(rows == cols, 1.25, 0.0).astype(jnp.float32)
    grads = [arrived_ref[slot] for slot in range(count)]
    factors = []
    for slot, grad in enumerate(grads):
        factors.append(
            left_ref[slot] + (1.0 - stat_decay) * product(grad, grad, ROWS_ROWS)
        )
        factors.append(
            right_ref[slot] + (1.0 - stat_decay) * product(grad, grad, COLS_COLS)
        )
    scales = [1.0 / (size_now * jnp.sqrt(mean_square(a) + eps_small)) for a in factors]
    starts = [a * s for a, s in zip(factors, scales)]
    firsts = [(diagonal - 0.25 * s).astype(jnp.bfloat16) for s in starts]
    starts = [s.astype(jnp.bfloat16) for s in starts]
    squares = [product(f, f).astype(jnp.bfloat16) for f in firsts]
    fourths = [product(s, s).astype(jnp.bfloat16) for s in squares]
    states = [product(f, s) for f, s in zip(fourths, starts)]
    seconds = [(diagonal - 0.25 * s).astype(jnp.bfloat16) for s in states]
    roots = [product(f, s).astype(jnp.bfloat16) for f, s in zip(firsts, seconds)]
    halves = [
        product(roots[2 * slot], grad).astype(jnp.bfloat16) for slot, grad in enumerate(grads)
    ]
    finals = [product(h, roots[2 * slot + 1]) for slot, h in enumerate(halves)]
    for slot, (grad, final) in enumerate(zip(grads, finals)):
        wide = grad.astype(jnp.float32)
        grad_norm = jnp.sqrt(mean_square(wide) + eps_small)
        cond_norm = jnp.sqrt(mean_square(final) + eps_small)
        fresh_ref[slot] = (final * (grad_norm / cond_norm)).astype(jnp.bfloat16)


def refresh(arrived, prev_left, prev_right):
    count, size_now, _ = arrived.shape
    return pl.pallas_call(
        refresh_kernel,
        out_shape=jax.ShapeDtypeStruct(arrived.shape, jnp.bfloat16),
        cost_estimate=pl.CostEstimate(
            flops=24 * count * size_now**3,
            bytes_accessed=12 * count * size_now**2,
            transcendentals=0,
        ),
        compiler_params=pltpu.CompilerParams(vmem_limit_bytes=VMEM_GRANT),
        name="refresh",
    )(arrived, prev_left, prev_right)


def part_kernel(place_ref, grads_ref, up_ref, down_ref, far_up_ref, far_down_ref, sems):
    residue = place_ref[0]
    half = far_up_ref.shape[0]
    pieces = (
        (slice(None), 1, up_ref),
        (slice(None), RADIX - 1, down_ref),
        (slice(0, half), 2, far_up_ref),
        (slice(half, None), 2, far_down_ref),
    )
    copies = [
        pltpu.make_async_copy(
            grads_ref.at[where, (residue + step) % RADIX], piece_ref, sems.at[index]
        )
        for index, (where, step, piece_ref) in enumerate(pieces)
    ]
    for copy in copies:
        copy.start()
    for copy in copies:
        copy.wait()


def part(residue, by_residue):
    count = by_residue.shape[0]
    pieces = [
        jax.ShapeDtypeStruct((size,) + by_residue.shape[2:], jnp.bfloat16)
        for size in (count, count, count // 2, count // 2)
    ]
    return pl.pallas_call(
        part_kernel,
        in_specs=[pl.BlockSpec(memory_space=pltpu.SMEM), pl.BlockSpec(memory_space=pltpu.HBM)],
        out_shape=pieces,
        out_specs=[pl.BlockSpec(memory_space=pltpu.VMEM)] * 4,
        scratch_shapes=[pltpu.SemaphoreType.DMA((4,))],
        compiler_params=pltpu.CompilerParams(vmem_limit_bytes=VMEM_GRANT),
        name="part",
    )(residue, pltpu.with_memory_space_constraint(by_residue, pltpu.HBM))


def combine_kernel(place_ref, grads_ref, up_ref, down_ref, far_up_ref, far_down_ref, out_ref):
    residue = place_ref[0]
    half = far_up_ref.shape[0]
    for index in range(2 * half):
        far_ref = far_up_ref if index < half else far_down_ref
        total = grads_ref[index, residue].astype(jnp.float32)
        total += up_ref[index].astype(jnp.float32)
        total += down_ref[index].astype(jnp.float32)
        total += far_ref[index % half].astype(jnp.float32)
        out_ref[index] = total.astype(jnp.bfloat16)


def combine(residue, by_residue, pieces):
    return pl.pallas_call(
        combine_kernel,
        in_specs=[pl.BlockSpec(memory_space=pltpu.SMEM)]
        + [pl.BlockSpec(memory_space=pltpu.VMEM)] * 5,
        out_shape=jax.ShapeDtypeStruct(pieces[0].shape, jnp.bfloat16),
        compiler_params=pltpu.CompilerParams(vmem_limit_bytes=VMEM_GRANT),
        name="combine",
    )(residue, by_residue, *pieces)


def gather_rows_kernel(table_ref, parts_ref, out_ref, sum_ref):
    total = parts_ref[0].astype(jnp.float32)
    for part in range(1, parts_ref.shape[0]):
        total += parts_ref[part].astype(jnp.float32)
    sum_ref[...] = total.astype(jnp.bfloat16)

    def step(slot, carry):
        out_ref[slot] = sum_ref[table_ref[slot]]
        return carry

    lax.fori_loop(0, out_ref.shape[0], step, 0, unroll=8)


def sum_and_gather(table, parts):
    count = table.shape[0]
    return pl.pallas_call(
        gather_rows_kernel,
        in_specs=[
            pl.BlockSpec(memory_space=pltpu.SMEM),
            pl.BlockSpec(memory_space=pltpu.VMEM),
        ],
        out_shape=jax.ShapeDtypeStruct((count,) + parts.shape[2:], jnp.bfloat16),
        scratch_shapes=[pltpu.VMEM(parts.shape[1:], jnp.bfloat16)],
        compiler_params=pltpu.CompilerParams(vmem_limit_bytes=VMEM_GRANT),
        name="sum_and_gather",
    )(table, parts)


def choose_kernel(picks_ref, returned_ref, chosen_ref):
    for block in range(chosen_ref.shape[0]):
        pick = picks_ref[block]
        found = returned_ref[jnp.maximum(pick, 0)]
        chosen_ref[block] = jnp.where(pick >= 0, found, jnp.zeros_like(found))


def choose(picks, returned):
    return pl.pallas_call(
        choose_kernel,
        in_specs=[
            pl.BlockSpec(memory_space=pltpu.SMEM),
            pl.BlockSpec(memory_space=pltpu.VMEM),
        ],
        out_shape=jax.ShapeDtypeStruct(picks.shape + returned.shape[1:], jnp.bfloat16),
        compiler_params=pltpu.CompilerParams(vmem_limit_bytes=VMEM_GRANT),
        name="choose",
    )(picks, returned)


def place_kernel(parity_ref, same_ref, low_ref, high_ref, out_ref, sems):
    parity = parity_ref[0]
    half = low_ref.shape[0]
    copies = [
        pltpu.make_async_copy(same_ref, out_ref.at[:, parity], sems.at[0]),
        pltpu.make_async_copy(low_ref, out_ref.at[:half, 1 - parity], sems.at[1]),
        pltpu.make_async_copy(high_ref, out_ref.at[half:, 1 - parity], sems.at[2]),
    ]
    for copy in copies:
        copy.start()
    for copy in copies:
        copy.wait()


def place(parity, same, low, high):
    return pl.pallas_call(
        place_kernel,
        in_specs=[pl.BlockSpec(memory_space=pltpu.SMEM)]
        + [pl.BlockSpec(memory_space=pltpu.VMEM)] * 3,
        out_specs=pl.BlockSpec(memory_space=pl.ANY),
        out_shape=jax.ShapeDtypeStruct((same.shape[0], 2) + same.shape[1:], jnp.bfloat16),
        scratch_shapes=[pltpu.SemaphoreType.DMA((3,))],
        compiler_params=pltpu.CompilerParams(vmem_limit_bytes=VMEM_GRANT),
        name="place",
    )(parity, same, low, high)


def shifted(value, step):
    size = lax.axis_size("dp")
    return lax.ppermute(value, "dp", [(i, (i + step) % size) for i in range(size)])


def strided(size, stride):
    return [list(range(start, size, stride)) for start in range(stride)]


def body(grads, owner_table, block_counts, prev_left, prev_right):
    owners = lax.axis_size("shard")
    groups = lax.axis_size("dp")
    my_group = lax.axis_index("dp")
    parity = my_group % 2
    blocks = grads.shape[1]
    row_count = grads.shape[2]
    block_width = grads.shape[3]
    per_group = blocks // groups
    half = groups // 4
    slot_total = owners * CAP
    slot_ids = jnp.arange(slot_total, dtype=jnp.int32)
    my_table = lax.dynamic_index_in_dim(owner_table, my_group, 0, keepdims=False)
    my_counts = lax.dynamic_index_in_dim(block_counts, my_group, 0, keepdims=False)
    is_live = (slot_ids % CAP).reshape(owners, CAP) < my_counts[:, None]
    is_live = is_live.reshape(slot_total)
    matches = (
        my_table[None, :] == jnp.arange(per_group, dtype=jnp.int32)[:, None]
    ) & is_live[None, :]
    earliest = jnp.min(jnp.where(matches, slot_ids[None, :], slot_total), axis=1)
    picks = jnp.where(earliest < slot_total, earliest, -1)

    residue = (my_group % RADIX).reshape(1)
    by_residue = grads.reshape(groups // RADIX, RADIX, per_group, row_count, block_width)
    up, down, far_up, far_down = part(residue, by_residue)
    pieces, my_table, picks, old_left, old_right = lax.optimization_barrier(
        (
            (shifted(up, 1), shifted(down, -1), shifted(far_up, 2), shifted(far_down, -2)),
            my_table,
            picks,
            stat_decay * prev_left,
            stat_decay * prev_right,
        )
    )
    parts = lax.all_to_all(
        combine(residue, by_residue, pieces),
        "dp",
        0,
        0,
        tiled=True,
        axis_index_groups=strided(groups, RADIX),
    )
    outgoing = sum_and_gather(my_table, parts)
    arrived = lax.all_to_all(
        outgoing.reshape(owners, CAP, row_count, block_width), "shard", 0, 0, tiled=True
    )
    arrived = jnp.swapaxes(arrived, 0, 1).reshape(CAP, block_width, block_width)
    fresh = refresh(arrived, old_left, old_right)
    fresh = jnp.swapaxes(fresh.reshape(CAP, owners, row_count, block_width), 0, 1)
    returned = lax.all_to_all(fresh, "shard", 0, 0, tiled=True)
    chosen = choose(picks, returned.reshape(slot_total, row_count, block_width))
    same = lax.all_gather(
        chosen, "dp", axis=0, tiled=False, axis_index_groups=strided(groups, 2)
    )
    low = shifted(same[:half], 1)
    high = shifted(same[half:], -1)
    placed = place(parity.reshape(1), same, low, high)
    return placed.reshape(blocks, row_count, block_width)


def solution(mesh):
    return jax.shard_map(
        body,
        mesh=mesh,
        in_specs=(
            P("dp", None, "shard", None),
            P(),
            P(),
            P(("dp", "shard"), None, None),
            P(("dp", "shard"), None, None),
        ),
        out_specs=P(None, "shard", None),
        check_vma=False,
    )
```

```python
import jax
import jax.numpy as jnp
from jax import lax
from jax.experimental import pallas as pl
from jax.experimental.pallas import tpu as pltpu
from jax.sharding import PartitionSpec as P

CAP = 2
RADIX = 4
VMEM_GRANT = 12 * 1024 * 1024


stat_decay = 0.9
eps_small = 1e-06

ROWS_ROWS = (((1,), (1,)), ((), ()))
COLS_COLS = (((0,), (0,)), ((), ()))


def product(left, right, dims=(((1,), (0,)), ((), ()))):
    return lax.dot_general(left, right, dims, preferred_element_type=jnp.float32)


def mean_square(value):
    return jnp.sum(value * value, keepdims=True) * (1.0 / value.size)


def refresh_kernel(arrived_ref, left_ref, right_ref, fresh_ref):
    count, size_now, _ = arrived_ref.shape
    rows = lax.broadcasted_iota(jnp.int32, (size_now, size_now), 0)
    cols = lax.broadcasted_iota(jnp.int32, (size_now, size_now), 1)
    diagonal = jnp.where(rows == cols, 1.25, 0.0).astype(jnp.float32)
    grads = [arrived_ref[slot] for slot in range(count)]
    factors = []
    for slot, grad in enumerate(grads):
        factors.append(
            left_ref[slot] + (1.0 - stat_decay) * product(grad, grad, ROWS_ROWS)
        )
        factors.append(
            right_ref[slot] + (1.0 - stat_decay) * product(grad, grad, COLS_COLS)
        )
    scales = [1.0 / (size_now * jnp.sqrt(mean_square(a) + eps_small)) for a in factors]
    starts = [a * s for a, s in zip(factors, scales)]
    firsts = [(diagonal - 0.25 * s).astype(jnp.bfloat16) for s in starts]
    starts = [s.astype(jnp.bfloat16) for s in starts]
    squares = [product(f, f).astype(jnp.bfloat16) for f in firsts]
    fourths = [product(s, s).astype(jnp.bfloat16) for s in squares]
    states = [product(f, s) for f, s in zip(fourths, starts)]
    seconds = [(diagonal - 0.25 * s).astype(jnp.bfloat16) for s in states]
    roots = [product(f, s).astype(jnp.bfloat16) for f, s in zip(firsts, seconds)]
    halves = [
        product(roots[2 * slot], grad).astype(jnp.bfloat16) for slot, grad in enumerate(grads)
    ]
    finals = [product(h, roots[2 * slot + 1]) for slot, h in enumerate(halves)]
    for slot, (grad, final) in enumerate(zip(grads, finals)):
        wide = grad.astype(jnp.float32)
        grad_norm = jnp.sqrt(mean_square(wide) + eps_small)
        cond_norm = jnp.sqrt(mean_square(final) + eps_small)
        fresh_ref[slot] = (final * (grad_norm / cond_norm)).astype(jnp.bfloat16)


def refresh(arrived, prev_left, prev_right):
    count, size_now, _ = arrived.shape
    return pl.pallas_call(
        refresh_kernel,
        out_shape=jax.ShapeDtypeStruct(arrived.shape, jnp.bfloat16),
        cost_estimate=pl.CostEstimate(
            flops=24 * count * size_now**3,
            bytes_accessed=12 * count * size_now**2,
            transcendentals=0,
        ),
        compiler_params=pltpu.CompilerParams(vmem_limit_bytes=VMEM_GRANT),
        name="refresh",
    )(arrived, prev_left, prev_right)


def part_kernel(place_ref, grads_ref, up_ref, down_ref, far_up_ref, far_down_ref, sems):
    residue = place_ref[0]
    half = far_up_ref.shape[0]
    pieces = (
        (slice(None), 1, up_ref),
        (slice(None), RADIX - 1, down_ref),
        (slice(0, half), 2, far_up_ref),
        (slice(half, None), 2, far_down_ref),
    )
    copies = [
        pltpu.make_async_copy(
            grads_ref.at[where, (residue + step) % RADIX], piece_ref, sems.at[index]
        )
        for index, (where, step, piece_ref) in enumerate(pieces)
    ]
    for copy in copies:
        copy.start()
    for copy in copies:
        copy.wait()


def part(residue, by_residue):
    count = by_residue.shape[0]
    pieces = [
        jax.ShapeDtypeStruct((size,) + by_residue.shape[2:], jnp.bfloat16)
        for size in (count, count, count // 2, count // 2)
    ]
    return pl.pallas_call(
        part_kernel,
        in_specs=[pl.BlockSpec(memory_space=pltpu.SMEM), pl.BlockSpec(memory_space=pltpu.HBM)],
        out_shape=pieces,
        out_specs=[pl.BlockSpec(memory_space=pltpu.VMEM)] * 4,
        scratch_shapes=[pltpu.SemaphoreType.DMA((4,))],
        compiler_params=pltpu.CompilerParams(vmem_limit_bytes=VMEM_GRANT),
        name="part",
    )(residue, pltpu.with_memory_space_constraint(by_residue, pltpu.HBM))


def combine_kernel(place_ref, grads_ref, up_ref, down_ref, far_up_ref, far_down_ref, out_ref):
    residue = place_ref[0]
    half = far_up_ref.shape[0]
    for index in range(2 * half):
        far_ref = far_up_ref if index < half else far_down_ref
        total = grads_ref[index, residue].astype(jnp.float32)
        total += up_ref[index].astype(jnp.float32)
        total += down_ref[index].astype(jnp.float32)
        total += far_ref[index % half].astype(jnp.float32)
        out_ref[index] = total.astype(jnp.bfloat16)


def combine(residue, by_residue, pieces):
    return pl.pallas_call(
        combine_kernel,
        in_specs=[pl.BlockSpec(memory_space=pltpu.SMEM)]
        + [pl.BlockSpec(memory_space=pltpu.VMEM)] * 5,
        out_shape=jax.ShapeDtypeStruct(pieces[0].shape, jnp.bfloat16),
        compiler_params=pltpu.CompilerParams(vmem_limit_bytes=VMEM_GRANT),
        name="combine",
    )(residue, by_residue, *pieces)


def gather_rows_kernel(table_ref, parts_ref, out_ref, sum_ref):
    total = parts_ref[0].astype(jnp.float32)
    for part in range(1, parts_ref.shape[0]):
        total += parts_ref[part].astype(jnp.float32)
    sum_ref[...] = total.astype(jnp.bfloat16)

    def step(slot, carry):
        out_ref[slot] = sum_ref[table_ref[slot]]
        return carry

    lax.fori_loop(0, out_ref.shape[0], step, 0, unroll=8)


def sum_and_gather(table, parts):
    count = table.shape[0]
    return pl.pallas_call(
        gather_rows_kernel,
        in_specs=[
            pl.BlockSpec(memory_space=pltpu.SMEM),
            pl.BlockSpec(memory_space=pltpu.VMEM),
        ],
        out_shape=jax.ShapeDtypeStruct((count,) + parts.shape[2:], jnp.bfloat16),
        scratch_shapes=[pltpu.VMEM(parts.shape[1:], jnp.bfloat16)],
        compiler_params=pltpu.CompilerParams(vmem_limit_bytes=VMEM_GRANT),
        name="sum_and_gather",
    )(table, parts)


def choose_kernel(picks_ref, returned_ref, chosen_ref):
    for block in range(chosen_ref.shape[0]):
        pick = picks_ref[block]
        found = returned_ref[jnp.maximum(pick, 0)]
        chosen_ref[block] = jnp.where(pick >= 0, found, jnp.zeros_like(found))


def choose(picks, returned):
    return pl.pallas_call(
        choose_kernel,
        in_specs=[
            pl.BlockSpec(memory_space=pltpu.SMEM),
            pl.BlockSpec(memory_space=pltpu.VMEM),
        ],
        out_shape=jax.ShapeDtypeStruct(picks.shape + returned.shape[1:], jnp.bfloat16),
        compiler_params=pltpu.CompilerParams(vmem_limit_bytes=VMEM_GRANT),
        name="choose",
    )(picks, returned)


def place_kernel(
    place_ref, same_ref, above_ref, below_ref, far_low_ref, far_high_ref, out_ref, sems
):
    residue = place_ref[0]
    half = far_low_ref.shape[0]
    pieces = (
        (slice(None), 0, same_ref),
        (slice(None), 1, above_ref),
        (slice(None), RADIX - 1, below_ref),
        (slice(0, half), 2, far_low_ref),
        (slice(half, None), 2, far_high_ref),
    )
    copies = [
        pltpu.make_async_copy(
            piece_ref, out_ref.at[where, (residue + step) % RADIX], sems.at[index]
        )
        for index, (where, step, piece_ref) in enumerate(pieces)
    ]
    for copy in copies:
        copy.start()
    for copy in copies:
        copy.wait()


def place(residue, same, *others):
    shape = (same.shape[0], RADIX) + same.shape[1:]
    return pl.pallas_call(
        place_kernel,
        in_specs=[pl.BlockSpec(memory_space=pltpu.SMEM)]
        + [pl.BlockSpec(memory_space=pltpu.VMEM)] * 5,
        out_specs=pl.BlockSpec(memory_space=pl.ANY),
        out_shape=jax.ShapeDtypeStruct(shape, jnp.bfloat16),
        scratch_shapes=[pltpu.SemaphoreType.DMA((5,))],
        compiler_params=pltpu.CompilerParams(vmem_limit_bytes=VMEM_GRANT),
        name="place",
    )(residue, same, *others)


def shifted(value, step):
    size = lax.axis_size("dp")
    return lax.ppermute(value, "dp", [(i, (i + step) % size) for i in range(size)])


def strided(size, stride):
    return [list(range(start, size, stride)) for start in range(stride)]


def body(grads, owner_table, block_counts, prev_left, prev_right):
    owners = lax.axis_size("shard")
    groups = lax.axis_size("dp")
    my_group = lax.axis_index("dp")
    blocks = grads.shape[1]
    row_count = grads.shape[2]
    block_width = grads.shape[3]
    per_group = blocks // groups
    half = groups // RADIX // 2
    slot_total = owners * CAP
    slot_ids = jnp.arange(slot_total, dtype=jnp.int32)
    my_table = lax.dynamic_index_in_dim(owner_table, my_group, 0, keepdims=False)
    my_counts = lax.dynamic_index_in_dim(block_counts, my_group, 0, keepdims=False)
    is_live = (slot_ids % CAP).reshape(owners, CAP) < my_counts[:, None]
    is_live = is_live.reshape(slot_total)
    matches = (
        my_table[None, :] == jnp.arange(per_group, dtype=jnp.int32)[:, None]
    ) & is_live[None, :]
    earliest = jnp.min(jnp.where(matches, slot_ids[None, :], slot_total), axis=1)
    picks = jnp.where(earliest < slot_total, earliest, -1)

    residue = (my_group % RADIX).reshape(1)
    by_residue = grads.reshape(groups // RADIX, RADIX, per_group, row_count, block_width)
    up, down, far_up, far_down = part(residue, by_residue)
    pieces, my_table, picks, old_left, old_right = lax.optimization_barrier(
        (
            (shifted(up, 1), shifted(down, -1), shifted(far_up, 2), shifted(far_down, -2)),
            my_table,
            picks,
            stat_decay * prev_left,
            stat_decay * prev_right,
        )
    )
    parts = lax.all_to_all(
        combine(residue, by_residue, pieces),
        "dp",
        0,
        0,
        tiled=True,
        axis_index_groups=strided(groups, RADIX),
    )
    outgoing = sum_and_gather(my_table, parts)
    arrived = lax.all_to_all(
        outgoing.reshape(owners, CAP, row_count, block_width), "shard", 0, 0, tiled=True
    )
    arrived = jnp.swapaxes(arrived, 0, 1).reshape(CAP, block_width, block_width)
    fresh = refresh(arrived, old_left, old_right)
    fresh = jnp.swapaxes(fresh.reshape(CAP, owners, row_count, block_width), 0, 1)
    returned = lax.all_to_all(fresh, "shard", 0, 0, tiled=True)
    chosen = choose(picks, returned.reshape(slot_total, row_count, block_width))
    same = lax.all_gather(
        chosen, "dp", axis=0, tiled=False, axis_index_groups=strided(groups, RADIX)
    )
    placed = place(
        residue,
        same,
        shifted(same, -1),
        shifted(same, 1),
        shifted(same[:half], 2),
        shifted(same[half:], -2),
    )
    return placed.reshape(blocks, row_count, block_width)


def solution(mesh):
    return jax.shard_map(
        body,
        mesh=mesh,
        in_specs=(
            P("dp", None, "shard", None),
            P(),
            P(),
            P(("dp", "shard"), None, None),
            P(("dp", "shard"), None, None),
        ),
        out_specs=P(None, "shard", None),
        check_vma=False,
    )
```

```python
import jax
import jax.numpy as jnp
from jax import lax
from jax.experimental import pallas as pl
from jax.experimental.pallas import tpu as pltpu
from jax.sharding import PartitionSpec as P

CAP = 2
RADIX = 4
VMEM_GRANT = 12 * 1024 * 1024


stat_decay = 0.9
eps_small = 1e-06

ROWS_ROWS = (((1,), (1,)), ((), ()))
COLS_COLS = (((0,), (0,)), ((), ()))


def product(left, right, dims=(((1,), (0,)), ((), ()))):
    return lax.dot_general(left, right, dims, preferred_element_type=jnp.float32)


def mean_square(value):
    return jnp.sum(value * value, keepdims=True) * (1.0 / value.size)


def refresh_kernel(arrived_ref, left_ref, right_ref, fresh_ref):
    count, size_now, _ = arrived_ref.shape
    rows = lax.broadcasted_iota(jnp.int32, (size_now, size_now), 0)
    cols = lax.broadcasted_iota(jnp.int32, (size_now, size_now), 1)
    diagonal = jnp.where(rows == cols, 1.25, 0.0).astype(jnp.float32)
    grads = [arrived_ref[slot] for slot in range(count)]
    factors = []
    for slot, grad in enumerate(grads):
        factors.append(
            left_ref[slot] + (1.0 - stat_decay) * product(grad, grad, ROWS_ROWS)
        )
        factors.append(
            right_ref[slot] + (1.0 - stat_decay) * product(grad, grad, COLS_COLS)
        )
    scales = [1.0 / (size_now * jnp.sqrt(mean_square(a) + eps_small)) for a in factors]
    starts = [a * s for a, s in zip(factors, scales)]
    firsts = [(diagonal - 0.25 * s).astype(jnp.bfloat16) for s in starts]
    starts = [s.astype(jnp.bfloat16) for s in starts]
    squares = [product(f, f).astype(jnp.bfloat16) for f in firsts]
    fourths = [product(s, s).astype(jnp.bfloat16) for s in squares]
    states = [product(f, s) for f, s in zip(fourths, starts)]
    seconds = [(diagonal - 0.25 * s).astype(jnp.bfloat16) for s in states]
    roots = [product(f, s).astype(jnp.bfloat16) for f, s in zip(firsts, seconds)]
    halves = [
        product(roots[2 * slot], grad).astype(jnp.bfloat16) for slot, grad in enumerate(grads)
    ]
    finals = [product(h, roots[2 * slot + 1]) for slot, h in enumerate(halves)]
    for slot, (grad, final) in enumerate(zip(grads, finals)):
        wide = grad.astype(jnp.float32)
        grad_norm = jnp.sqrt(mean_square(wide) + eps_small)
        cond_norm = jnp.sqrt(mean_square(final) + eps_small)
        fresh_ref[slot] = (final * (grad_norm / cond_norm)).astype(jnp.bfloat16)


def refresh(arrived, prev_left, prev_right):
    count, size_now, _ = arrived.shape
    return pl.pallas_call(
        refresh_kernel,
        out_shape=jax.ShapeDtypeStruct(arrived.shape, jnp.bfloat16),
        cost_estimate=pl.CostEstimate(
            flops=24 * count * size_now**3,
            bytes_accessed=12 * count * size_now**2,
            transcendentals=0,
        ),
        compiler_params=pltpu.CompilerParams(vmem_limit_bytes=VMEM_GRANT),
        name="refresh",
    )(arrived, prev_left, prev_right)


def part_kernel(place_ref, grads_ref, up_ref, down_ref, far_ref, sems):
    residue = place_ref[0]
    copies = [
        pltpu.make_async_copy(
            grads_ref.at[:, (residue + step) % RADIX], piece_ref, sems.at[index]
        )
        for index, (step, piece_ref) in enumerate(
            ((1, up_ref), (RADIX - 1, down_ref), (2, far_ref))
        )
    ]
    for copy in copies:
        copy.start()
    for copy in copies:
        copy.wait()


def part(residue, by_residue):
    piece = jax.ShapeDtypeStruct(
        by_residue.shape[:1] + by_residue.shape[2:], jnp.bfloat16
    )
    return pl.pallas_call(
        part_kernel,
        in_specs=[pl.BlockSpec(memory_space=pltpu.SMEM), pl.BlockSpec(memory_space=pltpu.HBM)],
        out_shape=[piece] * 3,
        out_specs=[pl.BlockSpec(memory_space=pltpu.VMEM)] * 3,
        scratch_shapes=[pltpu.SemaphoreType.DMA((3,))],
        compiler_params=pltpu.CompilerParams(vmem_limit_bytes=VMEM_GRANT),
        name="part",
    )(residue, pltpu.with_memory_space_constraint(by_residue, pltpu.HBM))


def combine_kernel(place_ref, grads_ref, up_ref, down_ref, far_ref, out_ref):
    residue = place_ref[0]
    for index in range(out_ref.shape[0]):
        total = grads_ref[index, residue].astype(jnp.float32)
        total += up_ref[index].astype(jnp.float32)
        total += down_ref[index].astype(jnp.float32)
        total += far_ref[index].astype(jnp.float32)
        out_ref[index] = total.astype(jnp.bfloat16)


def combine(residue, by_residue, pieces):
    return pl.pallas_call(
        combine_kernel,
        in_specs=[pl.BlockSpec(memory_space=pltpu.SMEM)]
        + [pl.BlockSpec(memory_space=pltpu.VMEM)] * 4,
        out_shape=jax.ShapeDtypeStruct(pieces[0].shape, jnp.bfloat16),
        compiler_params=pltpu.CompilerParams(vmem_limit_bytes=VMEM_GRANT),
        name="combine",
    )(residue, by_residue, *pieces)


def gather_rows_kernel(table_ref, parts_ref, out_ref, sum_ref):
    total = parts_ref[0].astype(jnp.float32)
    for part in range(1, parts_ref.shape[0]):
        total += parts_ref[part].astype(jnp.float32)
    sum_ref[...] = total.astype(jnp.bfloat16)

    def step(slot, carry):
        out_ref[slot] = sum_ref[table_ref[slot]]
        return carry

    lax.fori_loop(0, out_ref.shape[0], step, 0, unroll=8)


def sum_and_gather(table, parts):
    count = table.shape[0]
    return pl.pallas_call(
        gather_rows_kernel,
        in_specs=[
            pl.BlockSpec(memory_space=pltpu.SMEM),
            pl.BlockSpec(memory_space=pltpu.VMEM),
        ],
        out_shape=jax.ShapeDtypeStruct((count,) + parts.shape[2:], jnp.bfloat16),
        scratch_shapes=[pltpu.VMEM(parts.shape[1:], jnp.bfloat16)],
        compiler_params=pltpu.CompilerParams(vmem_limit_bytes=VMEM_GRANT),
        name="sum_and_gather",
    )(table, parts)


def choose_kernel(picks_ref, returned_ref, chosen_ref):
    for block in range(chosen_ref.shape[0]):
        pick = picks_ref[block]
        found = returned_ref[jnp.maximum(pick, 0)]
        chosen_ref[block] = jnp.where(pick >= 0, found, jnp.zeros_like(found))


def choose(picks, returned):
    return pl.pallas_call(
        choose_kernel,
        in_specs=[
            pl.BlockSpec(memory_space=pltpu.SMEM),
            pl.BlockSpec(memory_space=pltpu.VMEM),
        ],
        out_shape=jax.ShapeDtypeStruct(picks.shape + returned.shape[1:], jnp.bfloat16),
        compiler_params=pltpu.CompilerParams(vmem_limit_bytes=VMEM_GRANT),
        name="choose",
    )(picks, returned)


def place_kernel(place_ref, same_ref, above_ref, below_ref, far_ref, out_ref, sems):
    residue = place_ref[0]
    copies = [
        pltpu.make_async_copy(
            piece_ref, out_ref.at[:, (residue + step) % RADIX], sems.at[index]
        )
        for index, (step, piece_ref) in enumerate(
            ((0, same_ref), (1, above_ref), (RADIX - 1, below_ref), (2, far_ref))
        )
    ]
    for copy in copies:
        copy.start()
    for copy in copies:
        copy.wait()


def place(residue, same, *others):
    shape = (same.shape[0], RADIX) + same.shape[1:]
    return pl.pallas_call(
        place_kernel,
        in_specs=[pl.BlockSpec(memory_space=pltpu.SMEM)]
        + [pl.BlockSpec(memory_space=pltpu.VMEM)] * 4,
        out_specs=pl.BlockSpec(memory_space=pl.ANY),
        out_shape=jax.ShapeDtypeStruct(shape, jnp.bfloat16),
        scratch_shapes=[pltpu.SemaphoreType.DMA((4,))],
        compiler_params=pltpu.CompilerParams(vmem_limit_bytes=VMEM_GRANT),
        name="place",
    )(residue, same, *others)


def shifted(value, step):
    size = lax.axis_size("dp")
    return lax.ppermute(value, "dp", [(i, (i + step) % size) for i in range(size)])


def crossed(value):
    size = lax.axis_size("dp")
    pairs = [(i, (i + (-2 if i % 2 else 2)) % size) for i in range(size)]
    return lax.ppermute(value, "dp", pairs)


def strided(size, stride):
    return [list(range(start, size, stride)) for start in range(stride)]


def body(grads, owner_table, block_counts, prev_left, prev_right):
    owners = lax.axis_size("shard")
    groups = lax.axis_size("dp")
    my_group = lax.axis_index("dp")
    blocks = grads.shape[1]
    row_count = grads.shape[2]
    block_width = grads.shape[3]
    per_group = blocks // groups
    slot_total = owners * CAP
    slot_ids = jnp.arange(slot_total, dtype=jnp.int32)
    my_table = lax.dynamic_index_in_dim(owner_table, my_group, 0, keepdims=False)
    my_counts = lax.dynamic_index_in_dim(block_counts, my_group, 0, keepdims=False)
    is_live = (slot_ids % CAP).reshape(owners, CAP) < my_counts[:, None]
    is_live = is_live.reshape(slot_total)
    matches = (
        my_table[None, :] == jnp.arange(per_group, dtype=jnp.int32)[:, None]
    ) & is_live[None, :]
    earliest = jnp.min(jnp.where(matches, slot_ids[None, :], slot_total), axis=1)
    picks = jnp.where(earliest < slot_total, earliest, -1)

    residue = (my_group % RADIX).reshape(1)
    by_residue = grads.reshape(groups // RADIX, RADIX, per_group, row_count, block_width)
    up, down, far = part(residue, by_residue)
    pieces, my_table, picks, old_left, old_right = lax.optimization_barrier(
        (
            (shifted(up, 1), shifted(down, -1), crossed(far)),
            my_table,
            picks,
            stat_decay * prev_left,
            stat_decay * prev_right,
        )
    )
    parts = lax.all_to_all(
        combine(residue, by_residue, pieces),
        "dp",
        0,
        0,
        tiled=True,
        axis_index_groups=strided(groups, RADIX),
    )
    outgoing = sum_and_gather(my_table, parts)
    arrived = lax.all_to_all(
        outgoing.reshape(owners, CAP, row_count, block_width), "shard", 0, 0, tiled=True
    )
    arrived = jnp.swapaxes(arrived, 0, 1).reshape(CAP, block_width, block_width)
    fresh = refresh(arrived, old_left, old_right)
    fresh = jnp.swapaxes(fresh.reshape(CAP, owners, row_count, block_width), 0, 1)
    returned = lax.all_to_all(fresh, "shard", 0, 0, tiled=True)
    chosen = choose(picks, returned.reshape(slot_total, row_count, block_width))
    same = lax.all_gather(
        chosen, "dp", axis=0, tiled=False, axis_index_groups=strided(groups, RADIX)
    )
    placed = place(residue, same, shifted(same, -1), shifted(same, 1), crossed(same))
    return placed.reshape(blocks, row_count, block_width)


def solution(mesh):
    return jax.shard_map(
        body,
        mesh=mesh,
        in_specs=(
            P("dp", None, "shard", None),
            P(),
            P(),
            P(("dp", "shard"), None, None),
            P(("dp", "shard"), None, None),
        ),
        out_specs=P(None, "shard", None),
        check_vma=False,
    )
```

```python
import functools

import jax
import jax.numpy as jnp
from jax import lax
from jax.experimental import pallas as pl
from jax.experimental.pallas import tpu as pltpu
from jax.sharding import PartitionSpec as P

CAP = 2
RADIX = 4
VMEM_GRANT = 12 * 1024 * 1024


stat_decay = 0.9
eps_small = 1e-06

ROWS_ROWS = (((1,), (1,)), ((), ()))
COLS_COLS = (((0,), (0,)), ((), ()))


def product(left, right, dims=(((1,), (0,)), ((), ()))):
    return lax.dot_general(left, right, dims, preferred_element_type=jnp.float32)


def mean_square(value):
    return jnp.sum(value * value, keepdims=True) * (1.0 / value.size)


def refresh_kernel(arrived_ref, left_ref, right_ref, fresh_ref):
    count, size_now, _ = arrived_ref.shape
    rows = lax.broadcasted_iota(jnp.int32, (size_now, size_now), 0)
    cols = lax.broadcasted_iota(jnp.int32, (size_now, size_now), 1)
    diagonal = jnp.where(rows == cols, 1.25, 0.0).astype(jnp.float32)
    grads = [arrived_ref[slot] for slot in range(count)]
    factors = []
    for slot, grad in enumerate(grads):
        factors.append(
            left_ref[slot] + (1.0 - stat_decay) * product(grad, grad, ROWS_ROWS)
        )
        factors.append(
            right_ref[slot] + (1.0 - stat_decay) * product(grad, grad, COLS_COLS)
        )
    scales = [1.0 / (size_now * jnp.sqrt(mean_square(a) + eps_small)) for a in factors]
    starts = [a * s for a, s in zip(factors, scales)]
    firsts = [(diagonal - 0.25 * s).astype(jnp.bfloat16) for s in starts]
    starts = [s.astype(jnp.bfloat16) for s in starts]
    squares = [product(f, f).astype(jnp.bfloat16) for f in firsts]
    fourths = [product(s, s).astype(jnp.bfloat16) for s in squares]
    states = [product(f, s) for f, s in zip(fourths, starts)]
    seconds = [(diagonal - 0.25 * s).astype(jnp.bfloat16) for s in states]
    roots = [product(f, s).astype(jnp.bfloat16) for f, s in zip(firsts, seconds)]
    halves = [
        product(roots[2 * slot], grad).astype(jnp.bfloat16) for slot, grad in enumerate(grads)
    ]
    finals = [product(h, roots[2 * slot + 1]) for slot, h in enumerate(halves)]
    for slot, (grad, final) in enumerate(zip(grads, finals)):
        wide = grad.astype(jnp.float32)
        grad_norm = jnp.sqrt(mean_square(wide) + eps_small)
        cond_norm = jnp.sqrt(mean_square(final) + eps_small)
        fresh_ref[slot] = (final * (grad_norm / cond_norm)).astype(jnp.bfloat16)


def refresh(arrived, prev_left, prev_right):
    count, size_now, _ = arrived.shape
    return pl.pallas_call(
        refresh_kernel,
        out_shape=jax.ShapeDtypeStruct(arrived.shape, jnp.bfloat16),
        cost_estimate=pl.CostEstimate(
            flops=24 * count * size_now**3,
            bytes_accessed=12 * count * size_now**2,
            transcendentals=0,
        ),
        compiler_params=pltpu.CompilerParams(vmem_limit_bytes=VMEM_GRANT),
        name="refresh",
    )(arrived, prev_left, prev_right)


def part_kernel(steps, place_ref, grads_ref, *refs):
    residue = place_ref[0]
    piece_refs, sems = refs[-1 - len(steps) : -1], refs[-1]
    copies = [
        pltpu.make_async_copy(
            grads_ref.at[:, (residue + step) % RADIX], piece_ref, sems.at[index]
        )
        for index, (step, piece_ref) in enumerate(zip(steps, piece_refs))
    ]
    for copy in copies:
        copy.start()
    for copy in copies:
        copy.wait()


def part(residue, by_residue, steps, *after):
    piece = jax.ShapeDtypeStruct(
        by_residue.shape[:1] + by_residue.shape[2:], jnp.bfloat16
    )
    return pl.pallas_call(
        functools.partial(part_kernel, steps),
        in_specs=[pl.BlockSpec(memory_space=pltpu.SMEM), pl.BlockSpec(memory_space=pltpu.HBM)]
        + [pl.BlockSpec(memory_space=pl.ANY)] * len(after),
        out_shape=[piece] * len(steps),
        out_specs=[pl.BlockSpec(memory_space=pltpu.VMEM)] * len(steps),
        scratch_shapes=[pltpu.SemaphoreType.DMA((len(steps),))],
        compiler_params=pltpu.CompilerParams(vmem_limit_bytes=VMEM_GRANT),
        name="part",
    )(residue, pltpu.with_memory_space_constraint(by_residue, pltpu.HBM), *after)


def combine_kernel(place_ref, grads_ref, up_ref, down_ref, far_ref, out_ref):
    residue = place_ref[0]
    for index in range(out_ref.shape[0]):
        total = grads_ref[index, residue].astype(jnp.float32)
        total += up_ref[index].astype(jnp.float32)
        total += down_ref[index].astype(jnp.float32)
        total += far_ref[index].astype(jnp.float32)
        out_ref[index] = total.astype(jnp.bfloat16)


def combine(residue, by_residue, pieces):
    return pl.pallas_call(
        combine_kernel,
        in_specs=[pl.BlockSpec(memory_space=pltpu.SMEM)]
        + [pl.BlockSpec(memory_space=pltpu.VMEM)] * 4,
        out_shape=jax.ShapeDtypeStruct(pieces[0].shape, jnp.bfloat16),
        compiler_params=pltpu.CompilerParams(vmem_limit_bytes=VMEM_GRANT),
        name="combine",
    )(residue, by_residue, *pieces)


def gather_rows_kernel(table_ref, parts_ref, out_ref, sum_ref):
    total = parts_ref[0].astype(jnp.float32)
    for part in range(1, parts_ref.shape[0]):
        total += parts_ref[part].astype(jnp.float32)
    sum_ref[...] = total.astype(jnp.bfloat16)

    def step(slot, carry):
        out_ref[slot] = sum_ref[table_ref[slot]]
        return carry

    lax.fori_loop(0, out_ref.shape[0], step, 0, unroll=8)


def sum_and_gather(table, parts):
    count = table.shape[0]
    return pl.pallas_call(
        gather_rows_kernel,
        in_specs=[
            pl.BlockSpec(memory_space=pltpu.SMEM),
            pl.BlockSpec(memory_space=pltpu.VMEM),
        ],
        out_shape=jax.ShapeDtypeStruct((count,) + parts.shape[2:], jnp.bfloat16),
        scratch_shapes=[pltpu.VMEM(parts.shape[1:], jnp.bfloat16)],
        compiler_params=pltpu.CompilerParams(vmem_limit_bytes=VMEM_GRANT),
        name="sum_and_gather",
    )(table, parts)


def choose_kernel(picks_ref, returned_ref, chosen_ref):
    for block in range(chosen_ref.shape[0]):
        pick = picks_ref[block]
        found = returned_ref[jnp.maximum(pick, 0)]
        chosen_ref[block] = jnp.where(pick >= 0, found, jnp.zeros_like(found))


def choose(picks, returned):
    return pl.pallas_call(
        choose_kernel,
        in_specs=[
            pl.BlockSpec(memory_space=pltpu.SMEM),
            pl.BlockSpec(memory_space=pltpu.VMEM),
        ],
        out_shape=jax.ShapeDtypeStruct(picks.shape + returned.shape[1:], jnp.bfloat16),
        compiler_params=pltpu.CompilerParams(vmem_limit_bytes=VMEM_GRANT),
        name="choose",
    )(picks, returned)


def place_kernel(place_ref, same_ref, above_ref, below_ref, far_ref, out_ref, sems):
    residue = place_ref[0]
    copies = [
        pltpu.make_async_copy(
            piece_ref, out_ref.at[:, (residue + step) % RADIX], sems.at[index]
        )
        for index, (step, piece_ref) in enumerate(
            ((0, same_ref), (1, above_ref), (RADIX - 1, below_ref), (2, far_ref))
        )
    ]
    for copy in copies:
        copy.start()
    for copy in copies:
        copy.wait()


def place(residue, same, *others):
    shape = (same.shape[0], RADIX) + same.shape[1:]
    return pl.pallas_call(
        place_kernel,
        in_specs=[pl.BlockSpec(memory_space=pltpu.SMEM)]
        + [pl.BlockSpec(memory_space=pltpu.VMEM)] * 4,
        out_specs=pl.BlockSpec(memory_space=pl.ANY),
        out_shape=jax.ShapeDtypeStruct(shape, jnp.bfloat16),
        scratch_shapes=[pltpu.SemaphoreType.DMA((4,))],
        compiler_params=pltpu.CompilerParams(vmem_limit_bytes=VMEM_GRANT),
        name="place",
    )(residue, same, *others)


def shifted(value, step):
    size = lax.axis_size("dp")
    return lax.ppermute(value, "dp", [(i, (i + step) % size) for i in range(size)])


def crossed(value):
    size = lax.axis_size("dp")
    pairs = [(i, (i + (-2 if i % 2 else 2)) % size) for i in range(size)]
    return lax.ppermute(value, "dp", pairs)


def strided(size, stride):
    return [list(range(start, size, stride)) for start in range(stride)]


def body(grads, owner_table, block_counts, prev_left, prev_right):
    owners = lax.axis_size("shard")
    groups = lax.axis_size("dp")
    my_group = lax.axis_index("dp")
    blocks = grads.shape[1]
    row_count = grads.shape[2]
    block_width = grads.shape[3]
    per_group = blocks // groups
    slot_total = owners * CAP
    slot_ids = jnp.arange(slot_total, dtype=jnp.int32)
    my_table = lax.dynamic_index_in_dim(owner_table, my_group, 0, keepdims=False)
    my_counts = lax.dynamic_index_in_dim(block_counts, my_group, 0, keepdims=False)
    is_live = (slot_ids % CAP).reshape(owners, CAP) < my_counts[:, None]
    is_live = is_live.reshape(slot_total)
    matches = (
        my_table[None, :] == jnp.arange(per_group, dtype=jnp.int32)[:, None]
    ) & is_live[None, :]
    earliest = jnp.min(jnp.where(matches, slot_ids[None, :], slot_total), axis=1)
    picks = jnp.where(earliest < slot_total, earliest, -1)

    residue = (my_group % RADIX).reshape(1)
    by_residue = grads.reshape(groups // RADIX, RADIX, per_group, row_count, block_width)
    (far,) = part(residue, by_residue, (2,))
    up, down = part(residue, by_residue, (1, RADIX - 1), far)
    pieces, my_table, picks, old_left, old_right = lax.optimization_barrier(
        (
            (shifted(up, 1), shifted(down, -1), crossed(far)),
            my_table,
            picks,
            stat_decay * prev_left,
            stat_decay * prev_right,
        )
    )
    parts = lax.all_to_all(
        combine(residue, by_residue, pieces),
        "dp",
        0,
        0,
        tiled=True,
        axis_index_groups=strided(groups, RADIX),
    )
    outgoing = sum_and_gather(my_table, parts)
    arrived = lax.all_to_all(
        outgoing.reshape(owners, CAP, row_count, block_width), "shard", 0, 0, tiled=True
    )
    arrived = jnp.swapaxes(arrived, 0, 1).reshape(CAP, block_width, block_width)
    fresh = refresh(arrived, old_left, old_right)
    fresh = jnp.swapaxes(fresh.reshape(CAP, owners, row_count, block_width), 0, 1)
    returned = lax.all_to_all(fresh, "shard", 0, 0, tiled=True)
    chosen = choose(picks, returned.reshape(slot_total, row_count, block_width))
    same = lax.all_gather(
        chosen, "dp", axis=0, tiled=False, axis_index_groups=strided(groups, RADIX)
    )
    placed = place(residue, same, shifted(same, -1), shifted(same, 1), crossed(same))
    return placed.reshape(blocks, row_count, block_width)


def solution(mesh):
    return jax.shard_map(
        body,
        mesh=mesh,
        in_specs=(
            P("dp", None, "shard", None),
            P(),
            P(),
            P(("dp", "shard"), None, None),
            P(("dp", "shard"), None, None),
        ),
        out_specs=P(None, "shard", None),
        check_vma=False,
    )
```

```python
import functools

import jax
import jax.numpy as jnp
from jax import lax
from jax.experimental import pallas as pl
from jax.experimental.pallas import tpu as pltpu
from jax.sharding import PartitionSpec as P

CAP = 2
RADIX = 4
VMEM_GRANT = 12 * 1024 * 1024


stat_decay = 0.9
eps_small = 1e-06

ROWS_ROWS = (((1,), (1,)), ((), ()))
COLS_COLS = (((0,), (0,)), ((), ()))


def product(left, right, dims=(((1,), (0,)), ((), ()))):
    return lax.dot_general(left, right, dims, preferred_element_type=jnp.float32)


def mean_square(value):
    return jnp.sum(value * value, keepdims=True) * (1.0 / value.size)


def refresh_kernel(arrived_ref, left_ref, right_ref, fresh_ref):
    count, size_now, _ = arrived_ref.shape
    rows = lax.broadcasted_iota(jnp.int32, (size_now, size_now), 0)
    cols = lax.broadcasted_iota(jnp.int32, (size_now, size_now), 1)
    diagonal = jnp.where(rows == cols, 1.25, 0.0).astype(jnp.float32)
    grads = [arrived_ref[slot] for slot in range(count)]
    factors = []
    for slot, grad in enumerate(grads):
        factors.append(
            left_ref[slot] + (1.0 - stat_decay) * product(grad, grad, ROWS_ROWS)
        )
        factors.append(
            right_ref[slot] + (1.0 - stat_decay) * product(grad, grad, COLS_COLS)
        )
    scales = [1.0 / (size_now * jnp.sqrt(mean_square(a) + eps_small)) for a in factors]
    starts = [a * s for a, s in zip(factors, scales)]
    firsts = [(diagonal - 0.25 * s).astype(jnp.bfloat16) for s in starts]
    starts = [s.astype(jnp.bfloat16) for s in starts]
    squares = [product(f, f).astype(jnp.bfloat16) for f in firsts]
    fourths = [product(s, s).astype(jnp.bfloat16) for s in squares]
    states = [product(f, s) for f, s in zip(fourths, starts)]
    seconds = [(diagonal - 0.25 * s).astype(jnp.bfloat16) for s in states]
    roots = [product(f, s).astype(jnp.bfloat16) for f, s in zip(firsts, seconds)]
    halves = [
        product(roots[2 * slot], grad).astype(jnp.bfloat16) for slot, grad in enumerate(grads)
    ]
    finals = [product(h, roots[2 * slot + 1]) for slot, h in enumerate(halves)]
    for slot, (grad, final) in enumerate(zip(grads, finals)):
        wide = grad.astype(jnp.float32)
        grad_norm = jnp.sqrt(mean_square(wide) + eps_small)
        cond_norm = jnp.sqrt(mean_square(final) + eps_small)
        fresh_ref[slot] = (final * (grad_norm / cond_norm)).astype(jnp.bfloat16)


def refresh(arrived, prev_left, prev_right):
    count, size_now, _ = arrived.shape
    return pl.pallas_call(
        refresh_kernel,
        out_shape=jax.ShapeDtypeStruct(arrived.shape, jnp.bfloat16),
        cost_estimate=pl.CostEstimate(
            flops=24 * count * size_now**3,
            bytes_accessed=12 * count * size_now**2,
            transcendentals=0,
        ),
        compiler_params=pltpu.CompilerParams(vmem_limit_bytes=VMEM_GRANT),
        name="refresh",
    )(arrived, prev_left, prev_right)


def part_kernel(place_ref, grads_ref, up_ref, down_ref, far_ref, sems):
    residue = place_ref[0]
    copies = [
        pltpu.make_async_copy(
            grads_ref.at[:, (residue + step) % RADIX], piece_ref, sems.at[index]
        )
        for index, (step, piece_ref) in enumerate(
            ((1, up_ref), (RADIX - 1, down_ref), (2, far_ref))
        )
    ]
    for copy in copies:
        copy.start()
    for copy in copies:
        copy.wait()


def part(residue, by_residue):
    piece = jax.ShapeDtypeStruct(
        by_residue.shape[:1] + by_residue.shape[2:], jnp.bfloat16
    )
    return pl.pallas_call(
        part_kernel,
        in_specs=[pl.BlockSpec(memory_space=pltpu.SMEM), pl.BlockSpec(memory_space=pltpu.HBM)],
        out_shape=[piece] * 3,
        out_specs=[pl.BlockSpec(memory_space=pltpu.VMEM)] * 3,
        scratch_shapes=[pltpu.SemaphoreType.DMA((3,))],
        compiler_params=pltpu.CompilerParams(vmem_limit_bytes=VMEM_GRANT),
        name="part",
    )(residue, pltpu.with_memory_space_constraint(by_residue, pltpu.HBM))


def combine_kernel(place_ref, grads_ref, up_ref, down_ref, far_ref, out_ref):
    residue = place_ref[0]
    for index in range(out_ref.shape[0]):
        total = grads_ref[index, residue].astype(jnp.float32)
        total += up_ref[index].astype(jnp.float32)
        total += down_ref[index].astype(jnp.float32)
        total += far_ref[index].astype(jnp.float32)
        out_ref[index] = total.astype(jnp.bfloat16)


def combine(residue, by_residue, pieces):
    return pl.pallas_call(
        combine_kernel,
        in_specs=[pl.BlockSpec(memory_space=pltpu.SMEM)]
        + [pl.BlockSpec(memory_space=pltpu.VMEM)] * 4,
        out_shape=jax.ShapeDtypeStruct(pieces[0].shape, jnp.bfloat16),
        compiler_params=pltpu.CompilerParams(vmem_limit_bytes=VMEM_GRANT),
        name="combine",
    )(residue, by_residue, *pieces)


def gather_rows_kernel(table_ref, parts_ref, out_ref, sum_ref):
    total = parts_ref[0].astype(jnp.float32)
    for part in range(1, parts_ref.shape[0]):
        total += parts_ref[part].astype(jnp.float32)
    sum_ref[...] = total.astype(jnp.bfloat16)

    def step(slot, carry):
        out_ref[slot] = sum_ref[table_ref[slot]]
        return carry

    lax.fori_loop(0, out_ref.shape[0], step, 0, unroll=8)


def sum_and_gather(table, parts):
    count = table.shape[0]
    return pl.pallas_call(
        gather_rows_kernel,
        in_specs=[
            pl.BlockSpec(memory_space=pltpu.SMEM),
            pl.BlockSpec(memory_space=pltpu.VMEM),
        ],
        out_shape=jax.ShapeDtypeStruct((count,) + parts.shape[2:], jnp.bfloat16),
        scratch_shapes=[pltpu.VMEM(parts.shape[1:], jnp.bfloat16)],
        compiler_params=pltpu.CompilerParams(vmem_limit_bytes=VMEM_GRANT),
        name="sum_and_gather",
    )(table, parts)


def choose_kernel(picks_ref, returned_ref, chosen_ref):
    for block in range(chosen_ref.shape[0]):
        pick = picks_ref[block]
        found = returned_ref[jnp.maximum(pick, 0)]
        chosen_ref[block] = jnp.where(pick >= 0, found, jnp.zeros_like(found))


def choose(picks, returned):
    return pl.pallas_call(
        choose_kernel,
        in_specs=[
            pl.BlockSpec(memory_space=pltpu.SMEM),
            pl.BlockSpec(memory_space=pltpu.VMEM),
        ],
        out_shape=jax.ShapeDtypeStruct(picks.shape + returned.shape[1:], jnp.bfloat16),
        compiler_params=pltpu.CompilerParams(vmem_limit_bytes=VMEM_GRANT),
        name="choose",
    )(picks, returned)


def place_kernel(steps, place_ref, *refs):
    residue = place_ref[0]
    piece_refs, (out_ref, sems) = refs[: len(steps)], refs[-2:]
    copies = [
        pltpu.make_async_copy(
            piece_ref, out_ref.at[:, (residue + step) % RADIX], sems.at[index]
        )
        for index, (step, piece_ref) in enumerate(zip(steps, piece_refs))
    ]
    for copy in copies:
        copy.start()
    for copy in copies:
        copy.wait()


def place(residue, steps, pieces, *begun):
    shape = pieces[0].shape[:1] + (RADIX,) + pieces[0].shape[1:]
    return pl.pallas_call(
        functools.partial(place_kernel, steps),
        in_specs=[pl.BlockSpec(memory_space=pltpu.SMEM)]
        + [pl.BlockSpec(memory_space=pltpu.VMEM)] * len(pieces)
        + [pl.BlockSpec(memory_space=pl.ANY)] * len(begun),
        out_specs=pl.BlockSpec(memory_space=pl.ANY),
        out_shape=jax.ShapeDtypeStruct(shape, jnp.bfloat16),
        input_output_aliases={1 + len(pieces): 0} if begun else {},
        scratch_shapes=[pltpu.SemaphoreType.DMA((len(steps),))],
        compiler_params=pltpu.CompilerParams(vmem_limit_bytes=VMEM_GRANT),
        cost_estimate=pl.CostEstimate(
            flops=0,
            bytes_accessed=4 * len(pieces) * pieces[0].size,
            transcendentals=0,
        ),
        name="place",
    )(residue, *pieces, *begun)


def shifted(value, step):
    size = lax.axis_size("dp")
    return lax.ppermute(value, "dp", [(i, (i + step) % size) for i in range(size)])


def crossed(value):
    size = lax.axis_size("dp")
    pairs = [(i, (i + (-2 if i % 2 else 2)) % size) for i in range(size)]
    return lax.ppermute(value, "dp", pairs)


def strided(size, stride):
    return [list(range(start, size, stride)) for start in range(stride)]


def body(grads, owner_table, block_counts, prev_left, prev_right):
    owners = lax.axis_size("shard")
    groups = lax.axis_size("dp")
    my_group = lax.axis_index("dp")
    blocks = grads.shape[1]
    row_count = grads.shape[2]
    block_width = grads.shape[3]
    per_group = blocks // groups
    slot_total = owners * CAP
    slot_ids = jnp.arange(slot_total, dtype=jnp.int32)
    my_table = lax.dynamic_index_in_dim(owner_table, my_group, 0, keepdims=False)
    my_counts = lax.dynamic_index_in_dim(block_counts, my_group, 0, keepdims=False)
    is_live = (slot_ids % CAP).reshape(owners, CAP) < my_counts[:, None]
    is_live = is_live.reshape(slot_total)
    matches = (
        my_table[None, :] == jnp.arange(per_group, dtype=jnp.int32)[:, None]
    ) & is_live[None, :]
    earliest = jnp.min(jnp.where(matches, slot_ids[None, :], slot_total), axis=1)
    picks = jnp.where(earliest < slot_total, earliest, -1)

    residue = (my_group % RADIX).reshape(1)
    by_residue = grads.reshape(groups // RADIX, RADIX, per_group, row_count, block_width)
    up, down, far = part(residue, by_residue)
    pieces, my_table, picks, old_left, old_right = lax.optimization_barrier(
        (
            (shifted(up, 1), shifted(down, -1), crossed(far)),
            my_table,
            picks,
            stat_decay * prev_left,
            stat_decay * prev_right,
        )
    )
    parts = lax.all_to_all(
        combine(residue, by_residue, pieces),
        "dp",
        0,
        0,
        tiled=True,
        axis_index_groups=strided(groups, RADIX),
    )
    outgoing = sum_and_gather(my_table, parts)
    arrived = lax.all_to_all(
        outgoing.reshape(owners, CAP, row_count, block_width), "shard", 0, 0, tiled=True
    )
    arrived = jnp.swapaxes(arrived, 0, 1).reshape(CAP, block_width, block_width)
    fresh = refresh(arrived, old_left, old_right)
    fresh = jnp.swapaxes(fresh.reshape(CAP, owners, row_count, block_width), 0, 1)
    returned = lax.all_to_all(fresh, "shard", 0, 0, tiled=True)
    chosen = choose(picks, returned.reshape(slot_total, row_count, block_width))
    same = lax.all_gather(
        chosen, "dp", axis=0, tiled=False, axis_index_groups=strided(groups, RADIX)
    )
    near = (shifted(same, -1), shifted(same, 1))
    far = crossed(same)
    begun = place(residue, (0,), (same,))
    begun = place(residue, (2,), (far,), begun)
    placed = place(residue, (1, RADIX - 1), near, begun)
    return placed.reshape(blocks, row_count, block_width)


def solution(mesh):
    return jax.shard_map(
        body,
        mesh=mesh,
        in_specs=(
            P("dp", None, "shard", None),
            P(),
            P(),
            P(("dp", "shard"), None, None),
            P(("dp", "shard"), None, None),
        ),
        out_specs=P(None, "shard", None),
        check_vma=False,
    )
```

```python
import jax
import jax.numpy as jnp
from jax import lax
from jax.experimental import pallas as pl
from jax.experimental.pallas import tpu as pltpu
from jax.sharding import PartitionSpec as P

CAP = 2
RADIX = 4
VMEM_GRANT = 12 * 1024 * 1024


stat_decay = 0.9
eps_small = 1e-06

ROWS_ROWS = (((1,), (1,)), ((), ()))
COLS_COLS = (((0,), (0,)), ((), ()))


def product(left, right, dims=(((1,), (0,)), ((), ()))):
    return lax.dot_general(left, right, dims, preferred_element_type=jnp.float32)


def mean_square(value):
    return jnp.sum(value * value, keepdims=True) * (1.0 / value.size)


def refresh_kernel(arrived_ref, left_ref, right_ref, fresh_ref):
    count, size_now, _ = arrived_ref.shape
    rows = lax.broadcasted_iota(jnp.int32, (size_now, size_now), 0)
    cols = lax.broadcasted_iota(jnp.int32, (size_now, size_now), 1)
    diagonal = jnp.where(rows == cols, 1.25, 0.0).astype(jnp.float32)
    grads = [arrived_ref[slot] for slot in range(count)]
    factors = []
    for slot, grad in enumerate(grads):
        factors.append(
            left_ref[slot] + (1.0 - stat_decay) * product(grad, grad, ROWS_ROWS)
        )
        factors.append(
            right_ref[slot] + (1.0 - stat_decay) * product(grad, grad, COLS_COLS)
        )
    scales = [1.0 / (size_now * jnp.sqrt(mean_square(a) + eps_small)) for a in factors]
    starts = [a * s for a, s in zip(factors, scales)]
    firsts = [(diagonal - 0.25 * s).astype(jnp.bfloat16) for s in starts]
    starts = [s.astype(jnp.bfloat16) for s in starts]
    squares = [product(f, f).astype(jnp.bfloat16) for f in firsts]
    fourths = [product(s, s).astype(jnp.bfloat16) for s in squares]
    states = [product(f, s) for f, s in zip(fourths, starts)]
    seconds = [(diagonal - 0.25 * s).astype(jnp.bfloat16) for s in states]
    roots = [product(f, s).astype(jnp.bfloat16) for f, s in zip(firsts, seconds)]
    halves = [
        product(roots[2 * slot], grad).astype(jnp.bfloat16) for slot, grad in enumerate(grads)
    ]
    finals = [product(h, roots[2 * slot + 1]) for slot, h in enumerate(halves)]
    for slot, (grad, final) in enumerate(zip(grads, finals)):
        wide = grad.astype(jnp.float32)
        grad_norm = jnp.sqrt(mean_square(wide) + eps_small)
        cond_norm = jnp.sqrt(mean_square(final) + eps_small)
        fresh_ref[slot] = (final * (grad_norm / cond_norm)).astype(jnp.bfloat16)


def refresh(arrived, prev_left, prev_right):
    count, size_now, _ = arrived.shape
    return pl.pallas_call(
        refresh_kernel,
        out_shape=jax.ShapeDtypeStruct(arrived.shape, jnp.bfloat16),
        cost_estimate=pl.CostEstimate(
            flops=24 * count * size_now**3,
            bytes_accessed=12 * count * size_now**2,
            transcendentals=0,
        ),
        compiler_params=pltpu.CompilerParams(vmem_limit_bytes=VMEM_GRANT),
        name="refresh",
    )(arrived, prev_left, prev_right)


def part_kernel(place_ref, grads_ref, up_ref, down_ref, far_ref, sems):
    residue = place_ref[0]
    copies = [
        pltpu.make_async_copy(
            grads_ref.at[:, (residue + step) % RADIX], piece_ref, sems.at[index]
        )
        for index, (step, piece_ref) in enumerate(
            ((1, up_ref), (RADIX - 1, down_ref), (2, far_ref))
        )
    ]
    for copy in copies:
        copy.start()
    for copy in copies:
        copy.wait()


def part(residue, by_residue):
    piece = jax.ShapeDtypeStruct(
        by_residue.shape[:1] + by_residue.shape[2:], jnp.bfloat16
    )
    return pl.pallas_call(
        part_kernel,
        in_specs=[pl.BlockSpec(memory_space=pltpu.SMEM), pl.BlockSpec(memory_space=pltpu.HBM)],
        out_shape=[piece] * 3,
        out_specs=[pl.BlockSpec(memory_space=pltpu.VMEM)] * 3,
        scratch_shapes=[pltpu.SemaphoreType.DMA((3,))],
        compiler_params=pltpu.CompilerParams(vmem_limit_bytes=VMEM_GRANT),
        name="part",
    )(residue, pltpu.with_memory_space_constraint(by_residue, pltpu.HBM))


def combine_kernel(place_ref, grads_ref, up_ref, down_ref, far_ref, out_ref):
    residue = place_ref[0]
    for index in range(out_ref.shape[0]):
        total = grads_ref[index, residue].astype(jnp.float32)
        total += up_ref[index].astype(jnp.float32)
        total += down_ref[index].astype(jnp.float32)
        total += far_ref[index].astype(jnp.float32)
        out_ref[index] = total.astype(jnp.bfloat16)


def combine(residue, by_residue, pieces):
    return pl.pallas_call(
        combine_kernel,
        in_specs=[pl.BlockSpec(memory_space=pltpu.SMEM)]
        + [pl.BlockSpec(memory_space=pltpu.VMEM)] * 4,
        out_shape=jax.ShapeDtypeStruct(pieces[0].shape, jnp.bfloat16),
        compiler_params=pltpu.CompilerParams(vmem_limit_bytes=VMEM_GRANT),
        name="combine",
    )(residue, by_residue, *pieces)


def gather_rows_kernel(table_ref, parts_ref, out_ref, sum_ref):
    total = parts_ref[0].astype(jnp.float32)
    for part in range(1, parts_ref.shape[0]):
        total += parts_ref[part].astype(jnp.float32)
    sum_ref[...] = total.astype(jnp.bfloat16)

    def step(slot, carry):
        out_ref[slot] = sum_ref[table_ref[slot]]
        return carry

    lax.fori_loop(0, out_ref.shape[0], step, 0, unroll=32)


def sum_and_gather(table, parts):
    count = table.shape[0]
    return pl.pallas_call(
        gather_rows_kernel,
        in_specs=[
            pl.BlockSpec(memory_space=pltpu.SMEM),
            pl.BlockSpec(memory_space=pltpu.VMEM),
        ],
        out_shape=jax.ShapeDtypeStruct((count,) + parts.shape[2:], jnp.bfloat16),
        scratch_shapes=[pltpu.VMEM(parts.shape[1:], jnp.bfloat16)],
        compiler_params=pltpu.CompilerParams(vmem_limit_bytes=VMEM_GRANT),
        name="sum_and_gather",
    )(table, parts)


def choose_kernel(picks_ref, returned_ref, chosen_ref):
    for block in range(chosen_ref.shape[0]):
        pick = picks_ref[block]
        found = returned_ref[jnp.maximum(pick, 0)]
        chosen_ref[block] = jnp.where(pick >= 0, found, jnp.zeros_like(found))


def choose(picks, returned):
    return pl.pallas_call(
        choose_kernel,
        in_specs=[
            pl.BlockSpec(memory_space=pltpu.SMEM),
            pl.BlockSpec(memory_space=pltpu.VMEM),
        ],
        out_shape=jax.ShapeDtypeStruct(picks.shape + returned.shape[1:], jnp.bfloat16),
        compiler_params=pltpu.CompilerParams(vmem_limit_bytes=VMEM_GRANT),
        name="choose",
    )(picks, returned)


def place_kernel(place_ref, same_ref, above_ref, below_ref, far_ref, out_ref, sems):
    residue = place_ref[0]
    copies = [
        pltpu.make_async_copy(
            piece_ref, out_ref.at[:, (residue + step) % RADIX], sems.at[index]
        )
        for index, (step, piece_ref) in enumerate(
            ((0, same_ref), (1, above_ref), (RADIX - 1, below_ref), (2, far_ref))
        )
    ]
    for copy in copies:
        copy.start()
    for copy in copies:
        copy.wait()


def place(residue, same, *others):
    shape = (same.shape[0], RADIX) + same.shape[1:]
    return pl.pallas_call(
        place_kernel,
        in_specs=[pl.BlockSpec(memory_space=pltpu.SMEM)]
        + [pl.BlockSpec(memory_space=pltpu.VMEM)] * 4,
        out_specs=pl.BlockSpec(memory_space=pl.ANY),
        out_shape=jax.ShapeDtypeStruct(shape, jnp.bfloat16),
        scratch_shapes=[pltpu.SemaphoreType.DMA((4,))],
        compiler_params=pltpu.CompilerParams(vmem_limit_bytes=VMEM_GRANT),
        name="place",
    )(residue, same, *others)


def shifted(value, step):
    size = lax.axis_size("dp")
    return lax.ppermute(value, "dp", [(i, (i + step) % size) for i in range(size)])


def crossed(value):
    size = lax.axis_size("dp")
    pairs = [(i, (i + (-2 if i % 2 else 2)) % size) for i in range(size)]
    return lax.ppermute(value, "dp", pairs)


def strided(size, stride):
    return [list(range(start, size, stride)) for start in range(stride)]


def body(grads, owner_table, block_counts, prev_left, prev_right):
    owners = lax.axis_size("shard")
    groups = lax.axis_size("dp")
    my_group = lax.axis_index("dp")
    blocks = grads.shape[1]
    row_count = grads.shape[2]
    block_width = grads.shape[3]
    per_group = blocks // groups
    slot_total = owners * CAP
    slot_ids = jnp.arange(slot_total, dtype=jnp.int32)
    my_table = lax.dynamic_index_in_dim(owner_table, my_group, 0, keepdims=False)
    my_counts = lax.dynamic_index_in_dim(block_counts, my_group, 0, keepdims=False)
    is_live = (slot_ids % CAP).reshape(owners, CAP) < my_counts[:, None]
    is_live = is_live.reshape(slot_total)
    matches = (
        my_table[None, :] == jnp.arange(per_group, dtype=jnp.int32)[:, None]
    ) & is_live[None, :]
    earliest = jnp.min(jnp.where(matches, slot_ids[None, :], slot_total), axis=1)
    picks = jnp.where(earliest < slot_total, earliest, -1)

    residue = (my_group % RADIX).reshape(1)
    by_residue = grads.reshape(groups // RADIX, RADIX, per_group, row_count, block_width)
    up, down, far = part(residue, by_residue)
    pieces, my_table, picks, old_left, old_right = lax.optimization_barrier(
        (
            (shifted(up, 1), shifted(down, -1), crossed(far)),
            my_table,
            picks,
            stat_decay * prev_left,
            stat_decay * prev_right,
        )
    )
    parts = lax.all_to_all(
        combine(residue, by_residue, pieces),
        "dp",
        0,
        0,
        tiled=True,
        axis_index_groups=strided(groups, RADIX),
    )
    outgoing = sum_and_gather(my_table, parts)
    arrived = lax.all_to_all(
        outgoing.reshape(owners, CAP, row_count, block_width), "shard", 0, 0, tiled=True
    )
    arrived = jnp.swapaxes(arrived, 0, 1).reshape(CAP, block_width, block_width)
    fresh = refresh(arrived, old_left, old_right)
    fresh = jnp.swapaxes(fresh.reshape(CAP, owners, row_count, block_width), 0, 1)
    returned = lax.all_to_all(fresh, "shard", 0, 0, tiled=True)
    chosen = choose(picks, returned.reshape(slot_total, row_count, block_width))
    same = lax.all_gather(
        chosen, "dp", axis=0, tiled=False, axis_index_groups=strided(groups, RADIX)
    )
    placed = place(residue, same, shifted(same, -1), shifted(same, 1), crossed(same))
    return placed.reshape(blocks, row_count, block_width)


def solution(mesh):
    return jax.shard_map(
        body,
        mesh=mesh,
        in_specs=(
            P("dp", None, "shard", None),
            P(),
            P(),
            P(("dp", "shard"), None, None),
            P(("dp", "shard"), None, None),
        ),
        out_specs=P(None, "shard", None),
        check_vma=False,
    )
```
